32 devices in a mesh: grp: 2 (over x), reg: 16 (over z, y, core).
Axes of the slice: x: 2, y: 2, z: 4, core: 2. Of those that a mesh axis runs over, the one named last changes fastest.
Arguments:
- waveforms: bfloat16 [32, 3, 4096], P('grp', None, 'reg'), parts along dimension 0, may hold values from -6 to 6
- tail: bfloat16 [32, 3, 768], P('grp'), parts along dimension 0, may hold values from -6 to 6
- station_lists: int32 [32, 4], P('grp'), parts along dimension 0, may hold values from 0 to 15
- station_count: int32 [32], P(('grp', 'reg')), parts along dimension 0, may hold values from 1 to 4, 48 in all
- bank_of_region: int32 [32], P(('grp', 'reg')), parts along dimension 0, may hold values from 0 to 7
- library: bfloat16 [8, 16, 12, 512], replicated, may hold values from -0.25 to 0.25
- moveouts: int32 [32, 16, 12], P(('grp', 'reg')), parts along dimension 0, may hold values from 0 to 2
Outputs:
- detection: float32 [32, 4096], P('grp', 'reg'), parts along dimension 0
The draws below stay inside these ranges and needn't reach their ends.
There are 2 independent parts, one for each index of `grp`. The reference program is written for one: setup_inputs(seed, part) draws one part's arguments, and reference() takes and returns one part's arrays. A program takes and returns all parts, laid end to end along the dimension named above; an argument that names none is the same for every part. Nothing has to cross between parts.
All inputs are finite; a program needn't handle non-finite values. No bound on the sum of `station_count` on one device may be relied on, other than what follows from the above.
Results may differ from the reference program's by a relative error of at most 0.0003.
Values may be sent and summed in bfloat16 or wider, within the bound.
A program may use at most 64 MiB of HBM per device.

```python
import math
import jax
import jax.numpy as jnp
import numpy as np
from jax import lax

TAPS = 512
TEMPLATES = 16
SLOTS = 4
COMPS = 3
BANKS = 8
UNIT = 128
MOVE = 256
REGIONS = 16
STATIONS = 16
LENGTH = 4096
MARGIN = 768


def with_ends(drawn, rng, least, high):
    shape = drawn.shape
    spot = [jax.random.randint(jax.random.fold_in(rng, axis), (), 0, shape[axis]) for axis in range(len(shape))]
    drawn = drawn.at[tuple(spot)].set(least)
    longest = shape.index(max(shape))
    spot[longest] = (spot[longest] + 1) % shape[longest]
    return drawn.at[tuple(spot)].set(high)


def block_scale(own_key, extent, split, low, largest):
    gain = 1.0
    for axis_at, blocks in split:
        steps = jax.random.uniform(jax.random.fold_in(jax.random.fold_in(own_key, 6), axis_at), (blocks,), jnp.float32, low / len(split), largest / len(split))
        gain = gain * jnp.repeat(jnp.exp(steps), extent[axis_at] // blocks).reshape((-1,) + (1,) * (len(extent) - 1 - axis_at))
    return gain


def split_up(number_of, total, reach, lean):
    portions = [(1 << 20) // math.isqrt(grade ** lean) + 1 for grade in range(2, number_of + 1)]
    rest, holding = total - reach - (number_of - 1), [1] * (number_of - 1)
    while rest > 0:
        candidates = [i for i in range(number_of - 1) if holding[i] < reach]
        mass, remaining = sum([portions[i] for i in candidates]), rest
        for i in candidates:
            extra = min(reach - holding[i], max(1, remaining * portions[i] // mass), rest)
            holding[i] = holding[i] + extra
            rest = rest - extra
    return np.array([reach] + holding)


def ragged(own_key, number_of, total, most, lean):
    if number_of == 2:
        one = jax.random.randint(own_key, (), max(1, total - most), min(most, total - 1) + 1)
        return jnp.stack([one, total - one])
    tallies = jnp.asarray(split_up(number_of, total, most, lean), jnp.int32)
    twos = (number_of - 1) // 2
    giver, taker = tallies[1:1 + 2 * twos:2], tallies[2:2 + 2 * twos:2]
    margin = jnp.minimum(giver - 1, most - taker)
    passed = jax.random.randint(jax.random.fold_in(own_key, 1), (twos,), 0, 1 << 20) % (margin + 1)
    tallies = tallies.at[1:1 + 2 * twos:2].set(giver - passed).at[2:2 + 2 * twos:2].set(taker + passed)
    return tallies[jax.random.permutation(jax.random.fold_in(own_key, 2), number_of)]


def scatter_about(rng, extent, width, reach, shards=(), kind=jnp.bfloat16):
    level = block_scale(rng, extent, shards, -0.22, 0.18) if shards else 1.0
    array = jax.random.normal(rng, extent, jnp.float32) * width * level
    return jnp.minimum(jnp.maximum(array, -reach), reach).astype(kind)


def setup_inputs(seed: int = 0, part: int = 0) -> dict:
    keys = jax.random.split(jax.random.key(seed), 8)
    own_keys = jax.random.split(jax.random.fold_in(keys[7], part), 8)
    waveforms = scatter_about(own_keys[0], (STATIONS, COMPS, LENGTH), 1.0, 6.0, ((2, 16),))
    tail = scatter_about(own_keys[1], (STATIONS, COMPS, MARGIN), 1.0, 6.0)
    station_lists = with_ends(jax.random.randint(own_keys[2], (REGIONS, SLOTS), 0, STATIONS), jax.random.fold_in(own_keys[2], 1), 0, STATIONS - 1).astype(jnp.int32)
    station_count = ragged(own_keys[3], REGIONS, (SLOTS - 1) * REGIONS, SLOTS, 2).astype(jnp.int32)
    bank_of_region = with_ends(jax.random.randint(own_keys[4], (REGIONS,), 0, BANKS), jax.random.fold_in(own_keys[4], 1), 0, BANKS - 1).astype(jnp.int32)
    library = scatter_about(keys[5], (BANKS, TEMPLATES, SLOTS * COMPS, TAPS), TAPS ** -0.5, 0.25)
    moveouts = with_ends(jax.random.randint(own_keys[6], (REGIONS, TEMPLATES, SLOTS * COMPS), 0, MOVE // UNIT + 1), jax.random.fold_in(own_keys[6], 1), 0, (MOVE // UNIT + 1) - 1).astype(jnp.int32)
    return dict(waveforms=waveforms, tail=tail, station_lists=station_lists, station_count=station_count, bank_of_region=bank_of_region, library=library, moveouts=moveouts)


def reference(waveforms, tail, station_lists, station_count, bank_of_region, library, moveouts):
    complete = jnp.concatenate([waveforms, tail], axis=2)
    record_len = LENGTH + MARGIN
    out_len = LENGTH + MOVE
    fft_size = 1 << (record_len + TAPS).bit_length()
    channels = SLOTS * COMPS
    positions = jnp.arange(LENGTH, dtype=jnp.int32)

    def add_region(running, region):
        station_ids = lax.dynamic_index_in_dim(station_lists, region, 0, keepdims=False)
        signal = complete[station_ids].reshape(channels, record_len).astype(jnp.float32)
        bank_id = lax.dynamic_index_in_dim(bank_of_region, region, 0, keepdims=False)
        kernels = lax.dynamic_index_in_dim(library, bank_id, 0, keepdims=False).astype(jnp.float32)
        spectrum = jnp.fft.rfft(signal, fft_size)
        kernel_spec = jnp.fft.rfft(kernels, fft_size)
        correlation = jnp.fft.irfft(spectrum[None] * jnp.conj(kernel_spec), fft_size)[:, :, :out_len]
        squares = signal * signal
        cumulative = jnp.concatenate([jnp.zeros((channels, 1), squares.dtype), jnp.cumsum(squares, axis=1)], axis=1)
        energy = cumulative[:, TAPS:TAPS + out_len] - cumulative[:, :out_len]
        scaled = correlation / jnp.sqrt(energy / TAPS + 1e-05)[None]
        shifts = lax.dynamic_index_in_dim(moveouts, region, 0, keepdims=False)
        index = (shifts * UNIT).astype(jnp.int32)[:, :, None] + positions[None, None, :]
        shifted = jnp.take_along_axis(scaled, index, axis=2)
        count = lax.dynamic_index_in_dim(station_count, region, 0, keepdims=False)
        live_mask = (jnp.arange(channels, dtype=jnp.int32) // COMPS < count).astype(scaled.dtype)
        return (running + lax.optimization_barrier(jnp.sum(shifted * live_mask[None, :, None], axis=1)), None)
    start = jnp.zeros((TEMPLATES, LENGTH), jnp.float32)
    total, unused = lax.scan(add_region, start, jnp.arange(REGIONS, dtype=jnp.int32))
    return total / jnp.sqrt(jnp.float32(COMPS * SLOTS * REGIONS))
```

```python
import functools
import math

import jax
import jax.numpy as jnp
from jax import lax
from jax.experimental import pallas as pl
from jax.experimental.pallas import tpu as pltpu
from jax.sharding import PartitionSpec as P

UNIT = 128
GROUP = 16
MESH = pl.DeviceIdType.MESH


def lay(blocks, width):
    if width % UNIT == 0:
        return jnp.concatenate(blocks, axis=1)
    per = UNIT // width
    tiles = []
    for start in range(0, len(blocks), per):
        tile = blocks[start]
        for i, block in enumerate(blocks[start + 1:start + per]):
            tile = tile + pltpu.roll(block, (i + 1) * width, 1)
        tiles.append(tile)
    return jnp.concatenate(tiles, axis=1)


def padded(x, lanes):
    if x.shape[1] % lanes == 0:
        return x
    return jnp.concatenate([x, jnp.zeros((x.shape[0], lanes - x.shape[1] % lanes), x.dtype)], axis=1)


def kernel(n, taps, scale, wave_hbm, tail_hbm, lists_hbm, count_hbm, bank_hbm, lib_hbm, mov_hbm, out_ref,
           rec, lists, count, bank, lib, mov, mine, meta, movt, member, sums, fans, gain, hank0, hank1,
           local, tails, halo_send, halo_recv, meta_send, meta_recv):
    me = lax.axis_index("reg")
    pieces, comps, stations, piece = rec.shape
    halos = pieces - 1
    record = pieces * piece
    channels, _, templates = mov.shape
    regions = lists.shape[1]
    banks = lib.shape[1] // channels
    moves = (record - piece - taps) // UNIT + 1
    width = piece + (moves - 1) * UNIT
    rows = comps * stations
    packs = UNIT // templates
    groups = stations // GROUP

    loads = [pltpu.make_async_copy(src, dst, local.at[i]) for i, (src, dst) in enumerate((
        (mov_hbm, mov), (count_hbm, count), (bank_hbm, bank), (lists_hbm, lists), (wave_hbm, rec.at[0]),
        (lib_hbm, lib)))]
    for copy in loads:
        copy.start()

    def tail_copy(h, q):
        return pltpu.make_async_copy(tail_hbm.at[:, :, pl.ds(q * piece, piece)], rec.at[h], tails.at[h - 1])

    for h in range(1, halos + 1):
        for q in range(h):
            @pl.when(me + h - n == q)
            def _():
                tail_copy(h, q).start()

    barrier = pltpu.get_barrier_semaphore()

    @pl.loop(1, n)
    def _(step):
        pl.semaphore_signal(barrier, inc=1, device_id={"reg": lax.rem(me + step, n)}, device_id_type=MESH)

    for copy in loads[:3]:
        copy.wait()
    lane = lax.broadcasted_iota(jnp.int32, (1, UNIT), 1)
    live = jnp.broadcast_to(count[...], (1, UNIT))
    for q in range(2):
        spots = []
        for i in range(packs):
            c = q * packs + i
            if c < channels:
                row = padded(mov[c], UNIT)
                spots.append(jnp.where(lane < templates, jnp.where(c // comps < live, row, moves), 0))
            else:
                spots.append(jnp.where(lane < templates, jnp.broadcast_to(bank[...], (1, UNIT)), 0))
        mine[q:q + 1] = lay(spots, templates)

    def meta_copy(step):
        return pltpu.make_async_remote_copy(
            src_ref=mine, dst_ref=meta.at[me], send_sem=meta_send.at[step], recv_sem=meta_recv.at[step],
            device_id={"reg": lax.rem(me + step, n)}, device_id_type=MESH)

    def halo_copy(h):
        return pltpu.make_async_remote_copy(
            src_ref=rec.at[0], dst_ref=rec.at[h], send_sem=halo_send.at[h - 1], recv_sem=halo_recv.at[h - 1],
            device_id={"reg": lax.rem(me + n - h, n)}, device_id_type=MESH)

    for copy in loads[3:5]:
        copy.wait()

    blocks = []
    for i in range(packs):
        for q in range(2):
            c = q * packs + i
            if c < channels:
                blocks.append(padded(lists[c // comps:c // comps + 1] + 1, UNIT))
            else:
                blocks.append(jnp.zeros((1, max(regions, UNIT)), jnp.int32))
    listed = lay(blocks, regions)
    spot = lax.broadcasted_iota(jnp.int32, (GROUP, listed.shape[1]), 1) // regions
    channel = spot % 2 * packs + spot // 2

    def choose(base):
        station = lax.broadcasted_iota(jnp.int32, channel.shape, 0) + (base + 1)
        for c in range(comps):
            here = (jnp.broadcast_to(listed, channel.shape) == station) & (channel % comps == c)
            member[c] = jnp.where(here, 1.0, 0.0)

    if groups == 1:
        choose(0)

    pl.semaphore_wait(barrier, n - 1)

    @pl.loop(1, n)
    def _(step):
        meta_copy(step).start()

    for h in range(1, halos + 1):
        @pl.when(me >= h)
        def _():
            halo_copy(h).start()

    meta[me] = mine[...]
    loads[5].wait()

    @pl.loop(1, n)
    def _(step):
        meta_copy(step).wait_recv()

    told = jnp.concatenate([meta[:, q, :] for q in range(2)], axis=0).astype(jnp.float32)
    if 2 * regions % UNIT:
        told_full = jnp.concatenate([told, jnp.zeros((UNIT - 2 * regions, UNIT), jnp.float32)], axis=0)
    else:
        told_full = told
    turned = jnp.transpose(told_full)
    movt[...] = lay([turned[i * templates:(i + 1) * templates] for i in range(packs)], 2 * regions)

    high = told[regions:2 * regions]
    at = lax.broadcasted_iota(jnp.int32, high.shape, 1)
    used = jnp.where(at < UNIT // 2, pltpu.roll(high, UNIT // 2, 1), high)
    same = jnp.where(used == (at % banks).astype(jnp.float32), 1.0, 0.0)
    to_bank = jnp.concatenate([jnp.where(at // banks == q * packs + i, same, 0.0)
                               for i in range(packs) for q in range(2)], axis=0).astype(jnp.bfloat16)
    depth = lib.shape[1]

    def combine():
        for f in range(templates):
            moved = jnp.broadcast_to(movt[f:f + 1], channel.shape)
            picks = []
            for c in range(comps):
                for m in range(moves):
                    picks.append(jnp.where(moved == m, member[c], 0.0).astype(jnp.bfloat16))
            tally = jnp.dot(jnp.concatenate(picks, axis=0), to_bank, preferred_element_type=jnp.float32)
            bank_rows = jnp.concatenate([lib[f], jnp.zeros((UNIT - depth, taps), lib.dtype)], axis=0)
            total = jnp.dot(tally.astype(jnp.bfloat16), bank_rows, preferred_element_type=jnp.float32)
            for j in range(taps // UNIT):
                sums[j, pl.ds(f, total.shape[0], stride=templates)] = total[:, j * UNIT:(j + 1) * UNIT]

    if groups == 1:
        combine()

    for h in range(1, halos + 1):
        for q in range(h):
            @pl.when(me + h - n == q)
            def _():
                tail_copy(h, q).wait()

        @pl.when(me + h < n)
        def _():
            halo_copy(h).wait_recv()

    @pl.loop(0, stations, step=16)
    def _(s):
        s = pl.multiple_of(s, 16)
        for c in range(comps):
            x = jnp.concatenate([rec[p, c, pl.ds(s, 16)] for p in range(pieces)], axis=1).astype(jnp.float32)
            for k in range(8):
                at = pl.multiple_of(k * rows + c * stations + s, 16)
                moved = pltpu.roll(x, record - k, 1) if k else x
                for j in range(fans.shape[0]):
                    fans[j, pl.ds(at, 16)] = moved[:, j * UNIT:(j + 1) * UNIT]
            window = x * x
            span = 1
            while span < taps:
                window = window + pltpu.roll(window, record - span, 1)
                span *= 2
            at = pl.multiple_of(c * stations + s, 16)
            gain[pl.ds(at, 16)] = lax.rsqrt(window[:, 0:width] / taps + 1e-05) * scale

    def build(s, hank):
        for c in range(comps):
            fan = jnp.concatenate([fans[j, pl.ds(c * stations + s, 8, stride=rows)]
                                   for j in range(fans.shape[0])], axis=1)
            fan = jnp.concatenate([fan, pltpu.roll(fan, record - 8, 1)], axis=0).astype(jnp.bfloat16)
            for g in range(0, UNIT, 16):
                moved = (pltpu.roll(fan, record - g, 1) if g else fan).astype(jnp.bfloat16)
                hank[c, g:g + 16] = moved[:, 0:hank.shape[2]]

    def correlate(s, within, hank):
        total = None
        for c in range(comps):
            parts = []
            for m in range(moves):
                at = pl.multiple_of(((c * moves + m) * GROUP + within) * templates, templates)
                whole = jnp.concatenate([sums[j, pl.ds(at, templates)] for j in range(taps // UNIT)], axis=1)
                big = whole.astype(jnp.bfloat16)
                small = (whole - big.astype(jnp.float32)).astype(jnp.bfloat16)
                both = jnp.concatenate([big, small], axis=0)
                around = [both]
                if m:
                    around.insert(0, jnp.zeros((2 * templates, m * UNIT), jnp.bfloat16))
                if m < moves - 1:
                    around.append(jnp.zeros((2 * templates, (moves - 1 - m) * UNIT), jnp.bfloat16))
                parts.append(jnp.concatenate(around, axis=1))
            signal = jnp.concatenate([hank[c, :, i * UNIT:i * UNIT + piece]
                                      for i in range((width - piece + taps) // UNIT)], axis=0)
            corr = jnp.dot(jnp.concatenate(parts, axis=0), signal, preferred_element_type=jnp.float32)
            row = gain[pl.ds(c * stations + s, 1)]
            for m in range(moves):
                one = corr[2 * m * templates:(2 * m + 1) * templates] + corr[(2 * m + 1) * templates:(2 * m + 2) * templates]
                one = one * row[:, m * UNIT:m * UNIT + piece]
                total = one if total is None else total + one
        return total

    out_ref[...] = jnp.zeros_like(out_ref)
    build(0, hank0)

    @pl.loop(0, groups)
    def _(g):
        if groups > 1:
            choose(g * GROUP)
            combine()

        @pl.loop(0, GROUP, step=2)
        def _(within):
            s = g * GROUP + within
            first = correlate(s, within, hank0)
            build(s + 1, hank1)
            second = correlate(s + 1, within + 1, hank1)
            build(jnp.minimum(s + 2, stations - 1), hank0)
            out_ref[...] += first + second

    for h in range(1, halos + 1):
        @pl.when(me >= h)
        def _():
            halo_copy(h).wait_send()

    @pl.loop(1, n)
    def _(step):
        meta_copy(step).wait_send()


def on_device(waveforms, tail, station_lists, station_count, bank_of_region, library, moveouts):
    n = lax.axis_size("reg")
    stations, comps, piece = waveforms.shape
    banks, templates, channels, taps = library.shape
    regions, slots = station_lists.shape
    scale = 1.0 / math.sqrt(comps * slots * regions)
    pieces = 1 + tail.shape[2] // piece
    record = pieces * piece
    moves = (record - piece - taps) // UNIT + 1
    width = record - taps
    packs = UNIT // templates
    bank_rows = jnp.transpose(library, (1, 2, 0, 3)).reshape(templates, channels * banks, taps)
    anywhere = pl.BlockSpec(memory_space=pl.ANY)
    signal = pltpu.VMEM((comps, UNIT, record - UNIT), jnp.bfloat16)
    return pl.pallas_call(
        functools.partial(kernel, n, taps, scale),
        out_shape=jax.ShapeDtypeStruct((templates, piece), jnp.float32),
        in_specs=[anywhere] * 7,
        out_specs=pl.BlockSpec(memory_space=pltpu.VMEM),
        scratch_shapes=[
            pltpu.VMEM((pieces, comps, stations, piece), jnp.bfloat16),
            pltpu.VMEM((slots, regions), jnp.int32),
            pltpu.VMEM((1, 1), jnp.int32),
            pltpu.VMEM((1, 1), jnp.int32),
            pltpu.VMEM(bank_rows.shape, bank_rows.dtype),
            pltpu.VMEM((channels, 1, templates), jnp.int32),
            pltpu.VMEM((2, UNIT), jnp.int32),
            pltpu.VMEM((n, 2, UNIT), jnp.int32),
            pltpu.VMEM((templates, 2 * packs * regions), jnp.float32),
            pltpu.VMEM((comps, GROUP, 2 * packs * regions), jnp.float32),
            pltpu.VMEM((taps // UNIT, comps * moves * GROUP * templates, UNIT), jnp.float32),
            pltpu.VMEM((record // UNIT, 8 * comps * stations, UNIT), jnp.float32),
            pltpu.VMEM((comps * stations, width), jnp.float32),
            signal,
            signal,
            pltpu.SemaphoreType.DMA((6,)),
            pltpu.SemaphoreType.DMA((pieces - 1,)),
            pltpu.SemaphoreType.DMA((pieces - 1,)),
            pltpu.SemaphoreType.DMA((pieces - 1,)),
            pltpu.SemaphoreType.DMA((n,)),
            pltpu.SemaphoreType.DMA((n,)),
        ],
        compiler_params=pltpu.CompilerParams(collective_id=0, has_side_effects=True,
                                             vmem_limit_bytes=60 << 20),
        name="matched",
    )(jnp.transpose(waveforms, (1, 0, 2)), jnp.transpose(tail, (1, 0, 2)), station_lists.T,
      station_count.reshape(1, 1), bank_of_region.reshape(1, 1), bank_rows, jnp.transpose(moveouts, (2, 0, 1)))


def solution(mesh):
    return jax.shard_map(
        on_device,
        mesh=mesh,
        in_specs=(
            P("grp", None, "reg"),
            P("grp", None, None),
            P("grp", None),
            P(("grp", "reg")),
            P(("grp", "reg")),
            P(),
            P(("grp", "reg"), None, None),
        ),
        out_specs=P("grp", "reg"),
        check_vma=False,
    )
```

```python
import functools
import math

import jax
import jax.numpy as jnp
from jax import lax
from jax.experimental import pallas as pl
from jax.experimental.pallas import tpu as pltpu
from jax.sharding import PartitionSpec as P

UNIT = 128
GROUP = 16
SPAN = 4
STEP = 16
MESH = pl.DeviceIdType.MESH


def lay(blocks, width):
    if width % UNIT == 0:
        return jnp.concatenate(blocks, axis=1)
    per = UNIT // width
    tiles = []
    for start in range(0, len(blocks), per):
        tile = blocks[start]
        for i, block in enumerate(blocks[start + 1:start + per]):
            tile = tile + pltpu.roll(block, (i + 1) * width, 1)
        tiles.append(tile)
    return jnp.concatenate(tiles, axis=1)


def padded(x, lanes):
    if x.shape[1] % lanes == 0:
        return x
    return jnp.concatenate([x, jnp.zeros((x.shape[0], lanes - x.shape[1] % lanes), x.dtype)], axis=1)


def kernel(n, taps, scale, wave_hbm, tail_hbm, lists_hbm, count_hbm, bank_hbm, lib_hbm, mov_hbm, out_ref,
           rec, lists, count, bank, lib, mov, mine, meta, spread, band, member, tally, summed, fans, gain, partial,
           local, tails, halo_send, halo_recv, meta_send, meta_recv):
    me = lax.axis_index("reg")
    pieces, comps, stations, piece = rec.shape
    halos = pieces - 1
    record = pieces * piece
    channels, _, templates = mov.shape
    slots, regions = lists.shape
    quarters = taps // UNIT
    banks = lib.shape[1] // channels
    moves = (record - piece - taps) // UNIT + 1
    width = piece + (moves - 1) * UNIT
    pitch = comps * stations + 1
    packs = UNIT // templates
    groups = stations // GROUP

    barrier = pltpu.get_barrier_semaphore()
    loads = [pltpu.make_async_copy(src, dst, local.at[i]) for i, (src, dst) in enumerate(
        [(mov_hbm, mov), (count_hbm, count), (bank_hbm, bank), (lists_hbm, lists), (wave_hbm, rec.at[0])]
        + [(lib_hbm.at[:, :, j * UNIT:(j + 1) * UNIT], lib.at[j]) for j in range(quarters)])]

    for copy in loads[:5]:
        copy.start()

    @pl.loop(1, n)
    def _(step):
        pl.semaphore_signal(barrier, inc=1, device_id={"reg": lax.rem(me + step, n)}, device_id_type=MESH)

    def tail_copy(h, q):
        return pltpu.make_async_copy(tail_hbm.at[:, :, pl.ds(q * piece, piece)], rec.at[h], tails.at[h - 1])

    for h in range(1, halos + 1):
        for q in range(h):
            @pl.when(me + h - n == q)
            def _():
                tail_copy(h, q).start()

    for copy in loads[5:]:
        copy.start()
    for copy in loads[:3]:
        copy.wait()
    lane = lax.broadcasted_iota(jnp.int32, (1, UNIT), 1)
    live = jnp.broadcast_to(count[...].reshape(1, 1), (1, UNIT))
    for q in range(2):
        spots = []
        for i in range(packs):
            c = q * packs + i
            if c < channels:
                row = padded(mov[c], UNIT)
                spots.append(jnp.where(lane < templates, jnp.where(c // comps < live, row, moves), 0))
            else:
                spots.append(jnp.where(lane < templates, jnp.broadcast_to(bank[...].reshape(1, 1), (1, UNIT)), 0))
        mine[q:q + 1] = lay(spots, templates)

    def meta_copy(step):
        return pltpu.make_async_remote_copy(
            src_ref=mine, dst_ref=meta.at[me], send_sem=meta_send.at[step], recv_sem=meta_recv.at[step],
            device_id={"reg": lax.rem(me + step, n)}, device_id_type=MESH)

    def halo_copy(h):
        return pltpu.make_async_remote_copy(
            src_ref=rec.at[0], dst_ref=rec.at[h], send_sem=halo_send.at[h - 1], recv_sem=halo_recv.at[h - 1],
            device_id={"reg": lax.rem(me + n - h, n)}, device_id_type=MESH)

    for copy in loads[3:5]:
        copy.wait()

    def choose(base):
        station = lax.broadcasted_iota(jnp.int32, (GROUP, regions), 0) + base
        for k in range(slots):
            here = jnp.broadcast_to(lists[k:k + 1], station.shape) == station
            member[k] = jnp.where(here, 1.0, 0.0)

    if groups == 1:
        choose(0)

    pl.semaphore_wait(barrier, n - 1)

    @pl.loop(1, n)
    def _(step):
        meta_copy(step).start()

    for h in range(1, halos + 1):
        @pl.when(me >= h)
        def _():
            halo_copy(h).start()

    meta[me] = mine[...]
    source = lax.broadcasted_iota(jnp.int32, (UNIT, UNIT), 0)
    target = lax.broadcasted_iota(jnp.int32, (UNIT, UNIT), 1)
    for i in range(packs):
        spread[i] = jnp.where(source == target % templates + i * templates, 1.0, 0.0).astype(jnp.bfloat16)
    for i in range(quarters + 1):
        full = jnp.ones((UNIT, UNIT), jnp.float32)
        full = jnp.where(source >= target, full, 0.0) if i == 0 else full
        full = jnp.where(source < target, full, 0.0) if i == quarters else full
        band[i] = full.astype(jnp.bfloat16)
    for copy in loads[5:]:
        copy.wait()
    chunk = lax.broadcasted_iota(jnp.int32, (templates, UNIT), 1) // (UNIT // quarters)

    @pl.loop(0, lib.shape[1], unroll=12)
    def _(e):
        now = [lib[j, e] for j in range(quarters)]
        bit = quarters // 2
        while bit:
            first = chunk // bit % 2 == 0
            reach = bit * (UNIT // quarters)
            then = list(now)
            for j in range(quarters):
                if not j & bit:
                    then[j] = jnp.where(first, now[j], pltpu.roll(now[j + bit], reach, 1))
                    then[j + bit] = jnp.where(first, pltpu.roll(now[j], UNIT - reach, 1), now[j + bit])
            now = then
            bit //= 2
        for j in range(quarters):
            lib[j, e] = now[j]

    @pl.loop(1, n)
    def _(step):
        meta_copy(step).wait_recv()

    told = jnp.concatenate([meta[:, q, :] for q in range(2)], axis=0).astype(jnp.float32).astype(jnp.bfloat16)
    tiled = jnp.dot(told, jnp.concatenate([spread[i] for i in range(packs)], axis=1), preferred_element_type=jnp.float32)

    def facts(c):
        q, i = divmod(c, packs)
        return tiled[q * regions:(q + 1) * regions, i * UNIT:(i + 1) * UNIT]

    wide = lax.broadcasted_iota(jnp.int32, (regions, UNIT), 1) // templates
    home = facts(channels) == wide.astype(jnp.float32)

    def combine():
        for k in range(slots):
            parts = []
            for c in range(comps):
                shift = jnp.where(home, facts(k * comps + c), float(moves))
                for m in range(moves):
                    parts.append(jnp.where(shift == m, 1.0, 0.0).astype(jnp.bfloat16))
            many = jnp.dot(member[k].astype(jnp.bfloat16), jnp.concatenate(parts, axis=1),
                           preferred_element_type=jnp.float32)
            for i in range(comps * moves):
                tally[k, i] = many[:, i * UNIT:(i + 1) * UNIT]
        own = (lax.broadcasted_iota(jnp.int32, (templates, UNIT), 1) % templates
               == lax.broadcasted_iota(jnp.int32, (templates, UNIT), 0))

        @pl.loop(0, comps)
        def _(c):
            @pl.loop(0, GROUP, step=STEP)
            def _(base):
                picks = []
                for s in range(STEP):
                    for m in range(moves):
                        picks.append(jnp.concatenate([
                            jnp.where(own, jnp.broadcast_to(tally[k, c * moves + m, pl.ds(base + s, 1)], own.shape), 0.0)
                            .astype(jnp.bfloat16) for k in range(slots)], axis=1))
                weights = jnp.concatenate([
                    jnp.concatenate([lib[j, b * channels + k * comps + c] for j in range(quarters)], axis=1)
                    for k in range(slots) for b in range(banks)], axis=0)
                total = jnp.dot(jnp.concatenate(picks, axis=0), weights, preferred_element_type=jnp.float32)
                at = pl.multiple_of(base * (moves * templates), moves * templates)
                for j in range(quarters):
                    summed[c, j, pl.ds(at, STEP * moves * templates)] = total[:, j * UNIT:(j + 1) * UNIT]

    if groups == 1:
        combine()

    for h in range(1, halos + 1):
        for q in range(h):
            @pl.when(me + h - n == q)
            def _():
                tail_copy(h, q).wait()

        @pl.when(me + h < n)
        def _():
            halo_copy(h).wait_recv()

    @pl.loop(0, stations, step=16)
    def _(s):
        s = pl.multiple_of(s, 16)
        squares = []
        for c in range(comps):
            x = jnp.concatenate([rec[p, c, pl.ds(s, 16)] for p in range(pieces)], axis=1).astype(jnp.float32)
            for k in range(16):
                moved = pltpu.roll(x, record - k, 1) if k else x
                for j in range(fans.shape[0]):
                    fans[j, pl.ds(k * pitch + c * stations + s, 16)] = moved[:, j * UNIT:(j + 1) * UNIT]
            square = x * x
            big = square.astype(jnp.bfloat16)
            squares.append((big, (square - big.astype(jnp.float32)).astype(jnp.bfloat16)))
        both = jnp.concatenate([part[i] for i in range(2) for part in squares], axis=0)
        energy = jnp.dot(
            jnp.concatenate([both[:, a * UNIT:(a + quarters + 1) * UNIT] for a in range(width // UNIT)], axis=0),
            jnp.concatenate([band[i] for i in range(quarters + 1)], axis=0), preferred_element_type=jnp.float32)
        half = 16 * comps
        levels = []
        for a in range(width // UNIT):
            total = energy[2 * a * half:(2 * a + 1) * half] + energy[(2 * a + 1) * half:(2 * a + 2) * half]
            levels.append(lax.rsqrt(total / taps + 1e-05) * scale)
        level = jnp.concatenate(levels + levels[:1], axis=1)
        for i in range(quarters):
            moved = pltpu.roll(level, i * (UNIT // quarters), 1) if i else level
            for c in range(comps):
                for b in range(gain.shape[1]):
                    gain[i, b, pl.ds(c * stations + s, 16)] = moved[c * 16:(c + 1) * 16, b * UNIT:(b + 1) * UNIT]

    across = piece // UNIT

    def correlate(c, s, within, totals):
        low = jnp.concatenate([fans[j, pl.ds(c * stations + s, 16, stride=pitch)]
                               for j in range(fans.shape[0])], axis=1).astype(jnp.bfloat16)
        high = pltpu.roll(low, record - 16, 1)

        def signal(first, count):
            rows = [part[:, (j + first) * UNIT:(j + first + count) * UNIT] for j in range(quarters) for part in (low, high)]
            return jnp.concatenate(rows + rows, axis=0)

        kernels = []
        for m in range(moves):
            at = pl.multiple_of((within * moves + m) * templates, templates)
            for i in range(quarters):
                whole = summed[c, i, pl.ds(at, templates)]
                big = whole.astype(jnp.bfloat16)
                small = (whole - big.astype(jnp.float32)).astype(jnp.bfloat16)
                kernels.append(jnp.concatenate([big, small], axis=1))
        for first in range(0, moves + across, across):
            count = min(across, moves + across - first)
            wanted = [(m, i, q) for m in range(moves) for i in range(quarters)
                      for q in [[b for b in range(first, first + count) if 0 <= b - m < across + (i > 0)]] if q]
            corr = jnp.dot(jnp.concatenate([kernels[m * quarters + i] for m, i, _ in wanted], axis=0),
                           signal(first, count), preferred_element_type=jnp.float32)
            for at, (m, i, q) in enumerate(wanted):
                for b in q:
                    one = corr[at * templates:(at + 1) * templates, (b - first) * UNIT:(b - first + 1) * UNIT]
                    one = one * gain[i, b, pl.ds(c * stations + s, 1)]
                    old = totals.get((i, b - m))
                    totals[i, b - m] = one if old is None else old + one

    partial[...] = jnp.zeros_like(partial)

    @pl.loop(0, groups)
    def _(g):
        if groups > 1:
            choose(g * GROUP)
            combine()

        @pl.loop(0, GROUP, step=SPAN)
        def _(within):
            totals = {}
            for i in range(SPAN):
                for c in range(comps):
                    correlate(c, g * GROUP + within + i, within + i, totals)
            for (i, q), total in totals.items():
                partial[i, q] += total

    result = None
    for i in range(quarters):
        whole = jnp.concatenate([partial[i, q] for q in range(across + 1)], axis=1)
        whole = pltpu.roll(whole, whole.shape[1] - i * (UNIT // quarters), 1) if i else whole
        result = whole if result is None else result + whole
    out_ref[...] = result[:, 0:piece]

    for h in range(1, halos + 1):
        @pl.when(me >= h)
        def _():
            halo_copy(h).wait_send()

    @pl.loop(1, n)
    def _(step):
        meta_copy(step).wait_send()


def on_device(waveforms, tail, station_lists, station_count, bank_of_region, library, moveouts):
    n = lax.axis_size("reg")
    stations, comps, piece = waveforms.shape
    banks, templates, channels, taps = library.shape
    regions, slots = station_lists.shape
    scale = 1.0 / math.sqrt(comps * slots * regions)
    pieces = 1 + tail.shape[2] // piece
    record = pieces * piece
    moves = (record - piece - taps) // UNIT + 1
    width = record - taps
    packs = UNIT // templates
    bank_rows = jnp.transpose(library, (0, 2, 1, 3)).reshape(banks * channels, templates, taps)
    anywhere = pl.BlockSpec(memory_space=pltpu.HBM)
    return pl.pallas_call(
        functools.partial(kernel, n, taps, scale),
        out_shape=jax.ShapeDtypeStruct((templates, piece), jnp.float32),
        in_specs=[anywhere] * 7,
        out_specs=pl.BlockSpec(memory_space=pltpu.VMEM),
        scratch_shapes=[
            pltpu.VMEM((pieces, comps, stations, piece), jnp.bfloat16),
            pltpu.VMEM((slots, regions), jnp.int32),
            pltpu.VMEM((1,), jnp.int32),
            pltpu.VMEM((1,), jnp.int32),
            pltpu.VMEM((taps // UNIT, banks * channels, templates, UNIT), library.dtype),
            pltpu.VMEM((channels, 1, templates), jnp.int32),
            pltpu.VMEM((2, UNIT), jnp.int32),
            pltpu.VMEM((n, 2, UNIT), jnp.int32),
            pltpu.VMEM((packs, UNIT, UNIT), jnp.bfloat16),
            pltpu.VMEM((taps // UNIT + 1, UNIT, UNIT), jnp.bfloat16),
            pltpu.VMEM((slots, GROUP, regions), jnp.float32),
            pltpu.VMEM((slots, comps * moves, GROUP, UNIT), jnp.float32),
            pltpu.VMEM((comps, taps // UNIT, GROUP * moves * templates, UNIT), jnp.float32),
            pltpu.VMEM((record // UNIT, 16 * (comps * stations + 1), UNIT), jnp.float32),
            pltpu.VMEM((taps // UNIT, width // UNIT + 1, comps * stations, UNIT), jnp.float32),
            pltpu.VMEM((taps // UNIT, piece // UNIT + 1, templates, UNIT), jnp.float32),
            pltpu.SemaphoreType.DMA((5 + taps // UNIT,)),
            pltpu.SemaphoreType.DMA((pieces - 1,)),
            pltpu.SemaphoreType.DMA((pieces - 1,)),
            pltpu.SemaphoreType.DMA((pieces - 1,)),
            pltpu.SemaphoreType.DMA((n,)),
            pltpu.SemaphoreType.DMA((n,)),
        ],
        compiler_params=pltpu.CompilerParams(collective_id=0, has_side_effects=True,
                                             vmem_limit_bytes=60 << 20),
        name="matched",
    )(jnp.transpose(waveforms, (1, 0, 2)), jnp.transpose(tail, (1, 0, 2)), station_lists.T,
      station_count, bank_of_region, bank_rows, jnp.transpose(moveouts, (2, 0, 1)))


def solution(mesh):
    return jax.shard_map(
        on_device,
        mesh=mesh,
        in_specs=(
            P("grp", None, "reg"),
            P("grp", None, None),
            P("grp", None),
            P(("grp", "reg")),
            P(("grp", "reg")),
            P(),
            P(("grp", "reg"), None, None),
        ),
        out_specs=P("grp", "reg"),
        check_vma=False,
    )
```

```python
import functools
import math

import jax
import jax.numpy as jnp
from jax import lax
from jax.experimental import pallas as pl
from jax.experimental.pallas import tpu as pltpu
from jax.sharding import PartitionSpec as P

UNIT = 128
GROUP = 16
SPAN = 8
STEP = 16
MESH = pl.DeviceIdType.MESH


def lay(blocks, width):
    if width % UNIT == 0:
        return jnp.concatenate(blocks, axis=1)
    per = UNIT // width
    tiles = []
    for start in range(0, len(blocks), per):
        tile = blocks[start]
        for i, block in enumerate(blocks[start + 1:start + per]):
            tile = tile + pltpu.roll(block, (i + 1) * width, 1)
        tiles.append(tile)
    return jnp.concatenate(tiles, axis=1)


def padded(x, lanes):
    if x.shape[1] % lanes == 0:
        return x
    return jnp.concatenate([x, jnp.zeros((x.shape[0], lanes - x.shape[1] % lanes), x.dtype)], axis=1)


def kernel(n, taps, scale, wave_hbm, tail_hbm, lists_hbm, count_hbm, bank_hbm, lib_hbm, mov_hbm, out_ref,
           rec, lists, count, bank, lib, mov, mine, meta, spread, band, member, tally, summed, fans, gain, partial,
           local, tails, halo_send, halo_recv, meta_send, meta_recv):
    me = lax.axis_index("reg")
    pieces, comps, stations, piece = rec.shape
    halos = pieces - 1
    record = pieces * piece
    channels, _, templates = mov.shape
    slots, regions = lists.shape
    quarters = taps // UNIT
    banks = lib.shape[1] // channels
    moves = (record - piece - taps) // UNIT + 1
    width = piece + (moves - 1) * UNIT
    pitch = comps * stations + 1
    packs = UNIT // templates
    groups = stations // GROUP

    barrier = pltpu.get_barrier_semaphore()
    loads = [pltpu.make_async_copy(src, dst, local.at[i]) for i, (src, dst) in enumerate(
        [(mov_hbm, mov), (count_hbm, count), (bank_hbm, bank), (lists_hbm, lists), (wave_hbm, rec.at[0])]
        + [(lib_hbm.at[:, :, j * UNIT:(j + 1) * UNIT], lib.at[j]) for j in range(quarters)])]

    for copy in loads[:5]:
        copy.start()

    @pl.loop(1, n)
    def _(step):
        pl.semaphore_signal(barrier, inc=1, device_id={"reg": lax.rem(me + step, n)}, device_id_type=MESH)

    def tail_copy(h, q):
        return pltpu.make_async_copy(tail_hbm.at[:, :, pl.ds(q * piece, piece)], rec.at[h], tails.at[h - 1])

    for h in range(1, halos + 1):
        for q in range(h):
            @pl.when(me + h - n == q)
            def _():
                tail_copy(h, q).start()

    for copy in loads[5:]:
        copy.start()
    for copy in loads[:3]:
        copy.wait()
    lane = lax.broadcasted_iota(jnp.int32, (1, UNIT), 1)
    live = jnp.broadcast_to(count[...].reshape(1, 1), (1, UNIT))
    for q in range(2):
        spots = []
        for i in range(packs):
            c = q * packs + i
            if c < channels:
                row = padded(mov[c], UNIT)
                spots.append(jnp.where(lane < templates, jnp.where(c // comps < live, row, moves), 0))
            else:
                spots.append(jnp.where(lane < templates, jnp.broadcast_to(bank[...].reshape(1, 1), (1, UNIT)), 0))
        mine[q:q + 1] = lay(spots, templates)

    def meta_copy(step):
        return pltpu.make_async_remote_copy(
            src_ref=mine, dst_ref=meta.at[me], send_sem=meta_send, recv_sem=meta_recv,
            device_id={"reg": lax.rem(me + step, n)}, device_id_type=MESH)

    def halo_copy(h):
        return pltpu.make_async_remote_copy(
            src_ref=rec.at[0], dst_ref=rec.at[h], send_sem=halo_send.at[h - 1], recv_sem=halo_recv.at[h - 1],
            device_id={"reg": lax.rem(me + n - h, n)}, device_id_type=MESH)

    for copy in loads[3:5]:
        copy.wait()

    def choose(base):
        station = lax.broadcasted_iota(jnp.int32, (GROUP, regions), 0) + base
        for k in range(slots):
            here = jnp.broadcast_to(lists[k:k + 1], station.shape) == station
            member[k] = jnp.where(here, 1.0, 0.0)

    if groups == 1:
        choose(0)

    pl.semaphore_wait(barrier, n - 1)

    @pl.loop(1, n)
    def _(step):
        meta_copy(step).start()

    for h in range(1, halos + 1):
        @pl.when(me >= h)
        def _():
            halo_copy(h).start()

    meta[me] = mine[...]
    source = lax.broadcasted_iota(jnp.int32, (UNIT, UNIT), 0)
    target = lax.broadcasted_iota(jnp.int32, (UNIT, UNIT), 1)
    for i in range(packs):
        spread[i] = jnp.where(source == target % templates + i * templates, 1.0, 0.0).astype(jnp.bfloat16)
    for i in range(quarters + 1):
        full = jnp.ones((UNIT, UNIT), jnp.float32)
        full = jnp.where(source >= target, full, 0.0) if i == 0 else full
        full = jnp.where(source < target, full, 0.0) if i == quarters else full
        band[i] = full.astype(jnp.bfloat16)
    for copy in loads[5:]:
        copy.wait()
    chunk = lax.broadcasted_iota(jnp.int32, (templates, UNIT), 1) // (UNIT // quarters)

    @pl.loop(0, lib.shape[1], unroll=12)
    def _(e):
        now = [lib[j, e] for j in range(quarters)]
        bit = quarters // 2
        while bit:
            first = chunk // bit % 2 == 0
            reach = bit * (UNIT // quarters)
            then = list(now)
            for j in range(quarters):
                if not j & bit:
                    then[j] = jnp.where(first, now[j], pltpu.roll(now[j + bit], reach, 1))
                    then[j + bit] = jnp.where(first, pltpu.roll(now[j], UNIT - reach, 1), now[j + bit])
            now = then
            bit //= 2
        for j in range(quarters):
            lib[j, e] = now[j]

    everyone = meta.at[pl.ds(0, n - 1)]
    pltpu.make_async_copy(everyone, everyone, meta_recv).wait()

    told = jnp.concatenate([meta[:, q, :] for q in range(2)], axis=0).astype(jnp.float32).astype(jnp.bfloat16)
    tiled = jnp.dot(told, jnp.concatenate([spread[i] for i in range(packs)], axis=1), preferred_element_type=jnp.float32)

    def facts(c):
        q, i = divmod(c, packs)
        return tiled[q * regions:(q + 1) * regions, i * UNIT:(i + 1) * UNIT]

    wide = lax.broadcasted_iota(jnp.int32, (regions, UNIT), 1) // templates
    home = facts(channels) == wide.astype(jnp.float32)

    def combine():
        for k in range(slots):
            parts = []
            for c in range(comps):
                shift = jnp.where(home, facts(k * comps + c), float(moves))
                for m in range(moves):
                    parts.append(jnp.where(shift == m, 1.0, 0.0).astype(jnp.bfloat16))
            many = jnp.dot(member[k].astype(jnp.bfloat16), jnp.concatenate(parts, axis=1),
                           preferred_element_type=jnp.float32)
            for i in range(comps * moves):
                tally[k, i] = many[:, i * UNIT:(i + 1) * UNIT]
        own = (lax.broadcasted_iota(jnp.int32, (templates, UNIT), 1) % templates
               == lax.broadcasted_iota(jnp.int32, (templates, UNIT), 0))

        @pl.loop(0, comps)
        def _(c):
            @pl.loop(0, GROUP, step=STEP)
            def _(base):
                picks = []
                for s in range(STEP):
                    for m in range(moves):
                        picks.append(jnp.concatenate([
                            jnp.where(own, jnp.broadcast_to(tally[k, c * moves + m, pl.ds(base + s, 1)], own.shape), 0.0)
                            .astype(jnp.bfloat16) for k in range(slots)], axis=1))
                weights = jnp.concatenate([
                    jnp.concatenate([lib[j, b * channels + k * comps + c] for j in range(quarters)], axis=1)
                    for k in range(slots) for b in range(banks)], axis=0)
                total = jnp.dot(jnp.concatenate(picks, axis=0), weights, preferred_element_type=jnp.float32)
                at = pl.multiple_of(base * (moves * templates), moves * templates)
                for j in range(quarters):
                    summed[c, j, pl.ds(at, STEP * moves * templates)] = total[:, j * UNIT:(j + 1) * UNIT]

    if groups == 1:
        combine()

    for h in range(1, halos + 1):
        for q in range(h):
            @pl.when(me + h - n == q)
            def _():
                tail_copy(h, q).wait()

        @pl.when(me + h < n)
        def _():
            halo_copy(h).wait_recv()

    @pl.loop(0, stations, step=16)
    def _(s):
        s = pl.multiple_of(s, 16)
        squares = []
        for c in range(comps):
            x = jnp.concatenate([rec[p, c, pl.ds(s, 16)] for p in range(pieces)], axis=1).astype(jnp.float32)
            for k in range(16):
                moved = pltpu.roll(x, record - k, 1) if k else x
                for j in range(fans.shape[0]):
                    fans[j, pl.ds(k * pitch + c * stations + s, 16)] = moved[:, j * UNIT:(j + 1) * UNIT]
            square = x * x
            big = square.astype(jnp.bfloat16)
            squares.append((big, (square - big.astype(jnp.float32)).astype(jnp.bfloat16)))
        both = jnp.concatenate([part[i] for i in range(2) for part in squares], axis=0)
        energy = jnp.dot(
            jnp.concatenate([both[:, a * UNIT:(a + quarters + 1) * UNIT] for a in range(width // UNIT)], axis=0),
            jnp.concatenate([band[i] for i in range(quarters + 1)], axis=0), preferred_element_type=jnp.float32)
        half = 16 * comps
        levels = []
        for a in range(width // UNIT):
            total = energy[2 * a * half:(2 * a + 1) * half] + energy[(2 * a + 1) * half:(2 * a + 2) * half]
            levels.append(lax.rsqrt(total / taps + 1e-05) * scale)
        level = jnp.concatenate(levels + levels[:1], axis=1)
        for i in range(quarters):
            moved = pltpu.roll(level, i * (UNIT // quarters), 1) if i else level
            for c in range(comps):
                for b in range(gain.shape[1]):
                    gain[i, b, pl.ds(c * stations + s, 16)] = moved[c * 16:(c + 1) * 16, b * UNIT:(b + 1) * UNIT]

    across = piece // UNIT

    def correlate(c, s, within, totals):
        low = jnp.concatenate([fans[j, pl.ds(c * stations + s, 16, stride=pitch)]
                               for j in range(fans.shape[0])], axis=1).astype(jnp.bfloat16)
        high = pltpu.roll(low, record - 16, 1)

        def signal(first, count):
            rows = [part[:, (j + first) * UNIT:(j + first + count) * UNIT] for j in range(quarters) for part in (low, high)]
            return jnp.concatenate(rows + rows, axis=0)

        kernels = []
        for m in range(moves):
            at = pl.multiple_of((within * moves + m) * templates, templates)
            for i in range(quarters):
                whole = summed[c, i, pl.ds(at, templates)]
                big = whole.astype(jnp.bfloat16)
                small = (whole - big.astype(jnp.float32)).astype(jnp.bfloat16)
                kernels.append(jnp.concatenate([big, small], axis=1))
        for first in range(0, moves + across, across):
            count = min(across, moves + across - first)
            wanted = [(m, i, q) for m in range(moves) for i in range(quarters)
                      for q in [[b for b in range(first, first + count) if 0 <= b - m < across + (i > 0)]] if q]
            corr = jnp.dot(jnp.concatenate([kernels[m * quarters + i] for m, i, _ in wanted], axis=0),
                           signal(first, count), preferred_element_type=jnp.float32)
            for at, (m, i, q) in enumerate(wanted):
                for b in q:
                    one = corr[at * templates:(at + 1) * templates, (b - first) * UNIT:(b - first + 1) * UNIT]
                    one = one * gain[i, b, pl.ds(c * stations + s, 1)]
                    old = totals.get((i, b - m))
                    totals[i, b - m] = one if old is None else old + one

    partial[...] = jnp.zeros_like(partial)

    @pl.loop(0, groups)
    def _(g):
        if groups > 1:
            choose(g * GROUP)
            combine()

        @pl.loop(0, GROUP, step=SPAN)
        def _(within):
            totals = {}
            for i in range(SPAN):
                for c in range(comps):
                    correlate(c, g * GROUP + within + i, within + i, totals)
            for (i, q), total in totals.items():
                partial[i, q] += total

    result = None
    for i in range(quarters):
        whole = jnp.concatenate([partial[i, q] for q in range(across + 1)], axis=1)
        whole = pltpu.roll(whole, whole.shape[1] - i * (UNIT // quarters), 1) if i else whole
        result = whole if result is None else result + whole
    out_ref[...] = result[:, 0:piece]

    for h in range(1, halos + 1):
        @pl.when(me >= h)
        def _():
            halo_copy(h).wait_send()

    pltpu.make_async_copy(everyone, everyone, meta_send).wait()


def on_device(waveforms, tail, station_lists, station_count, bank_of_region, library, moveouts):
    n = lax.axis_size("reg")
    stations, comps, piece = waveforms.shape
    banks, templates, channels, taps = library.shape
    regions, slots = station_lists.shape
    scale = 1.0 / math.sqrt(comps * slots * regions)
    pieces = 1 + tail.shape[2] // piece
    record = pieces * piece
    moves = (record - piece - taps) // UNIT + 1
    width = record - taps
    packs = UNIT // templates
    bank_rows = jnp.transpose(library, (0, 2, 1, 3)).reshape(banks * channels, templates, taps)
    anywhere = pl.BlockSpec(memory_space=pltpu.HBM)
    return pl.pallas_call(
        functools.partial(kernel, n, taps, scale),
        out_shape=jax.ShapeDtypeStruct((templates, piece), jnp.float32),
        in_specs=[anywhere] * 7,
        out_specs=pl.BlockSpec(memory_space=pltpu.VMEM),
        scratch_shapes=[
            pltpu.VMEM((pieces, comps, stations, piece), jnp.bfloat16),
            pltpu.VMEM((slots, regions), jnp.int32),
            pltpu.VMEM((1,), jnp.int32),
            pltpu.VMEM((1,), jnp.int32),
            pltpu.VMEM((taps // UNIT, banks * channels, templates, UNIT), library.dtype),
            pltpu.VMEM((channels, 1, templates), jnp.int32),
            pltpu.VMEM((2, UNIT), jnp.int32),
            pltpu.VMEM((n, 2, UNIT), jnp.int32),
            pltpu.VMEM((packs, UNIT, UNIT), jnp.bfloat16),
            pltpu.VMEM((taps // UNIT + 1, UNIT, UNIT), jnp.bfloat16),
            pltpu.VMEM((slots, GROUP, regions), jnp.float32),
            pltpu.VMEM((slots, comps * moves, GROUP, UNIT), jnp.float32),
            pltpu.VMEM((comps, taps // UNIT, GROUP * moves * templates, UNIT), jnp.float32),
            pltpu.VMEM((record // UNIT, 16 * (comps * stations + 1), UNIT), jnp.float32),
            pltpu.VMEM((taps // UNIT, width // UNIT + 1, comps * stations, UNIT), jnp.float32),
            pltpu.VMEM((taps // UNIT, piece // UNIT + 1, templates, UNIT), jnp.float32),
            pltpu.SemaphoreType.DMA((5 + taps // UNIT,)),
            pltpu.SemaphoreType.DMA((pieces - 1,)),
            pltpu.SemaphoreType.DMA((pieces - 1,)),
            pltpu.SemaphoreType.DMA((pieces - 1,)),
            pltpu.SemaphoreType.DMA,
            pltpu.SemaphoreType.DMA,
        ],
        compiler_params=pltpu.CompilerParams(collective_id=0, has_side_effects=True,
                                             vmem_limit_bytes=60 << 20),
        name="matched",
    )(jnp.transpose(waveforms, (1, 0, 2)), jnp.transpose(tail, (1, 0, 2)), station_lists.T,
      station_count, bank_of_region, bank_rows, jnp.transpose(moveouts, (2, 0, 1)))


def solution(mesh):
    return jax.shard_map(
        on_device,
        mesh=mesh,
        in_specs=(
            P("grp", None, "reg"),
            P("grp", None, None),
            P("grp", None),
            P(("grp", "reg")),
            P(("grp", "reg")),
            P(),
            P(("grp", "reg"), None, None),
        ),
        out_specs=P("grp", "reg"),
        check_vma=False,
    )
```

```python
import functools
import math

import jax
import jax.numpy as jnp
from jax import lax
from jax.experimental import pallas as pl
from jax.experimental.pallas import tpu as pltpu
from jax.sharding import PartitionSpec as P

UNIT = 128
GROUP = 16
SPAN = 8
MESH = pl.DeviceIdType.MESH


def lay(blocks, width):
    if width % UNIT == 0:
        return jnp.concatenate(blocks, axis=1)
    per = UNIT // width
    tiles = []
    for start in range(0, len(blocks), per):
        tile = blocks[start]
        for i, block in enumerate(blocks[start + 1:start + per]):
            tile = tile + pltpu.roll(block, (i + 1) * width, 1)
        tiles.append(tile)
    return jnp.concatenate(tiles, axis=1)


def padded(x, lanes):
    if x.shape[1] % lanes == 0:
        return x
    return jnp.concatenate([x, jnp.zeros((x.shape[0], lanes - x.shape[1] % lanes), x.dtype)], axis=1)


def kernel(n, taps, scale, wave_hbm, tail_hbm, lists_hbm, count_hbm, bank_hbm, lib_hbm, mov_hbm, out_ref,
           rec, lists, count, bank, lib, mov, mine, meta, spread, band, member, tally, summed, fans, gain, partial,
           local, tails, halo_send, halo_recv, meta_send, meta_recv):
    me = lax.axis_index("reg")
    pieces, comps, stations, piece = rec.shape
    halos = pieces - 1
    record = pieces * piece
    channels, _, templates = mov.shape
    slots, regions = lists.shape
    quarters = taps // UNIT
    banks = lib.shape[1] // channels
    moves = (record - piece - taps) // UNIT + 1
    width = piece + (moves - 1) * UNIT
    pitch = comps * stations + 1
    packs = UNIT // templates
    sides = slots // 2
    half = templates // 2
    groups = stations // GROUP

    barrier = pltpu.get_barrier_semaphore()
    loads = [pltpu.make_async_copy(src, dst, local.at[i]) for i, (src, dst) in enumerate(
        [(mov_hbm, mov), (count_hbm, count), (bank_hbm, bank), (lists_hbm, lists), (wave_hbm, rec.at[0])]
        + [(lib_hbm.at[:, :, j * UNIT:(j + 1) * UNIT], lib.at[j]) for j in range(quarters)])]

    for copy in loads[:5]:
        copy.start()

    @pl.loop(1, n)
    def _(step):
        pl.semaphore_signal(barrier, inc=1, device_id={"reg": lax.rem(me + step, n)}, device_id_type=MESH)

    def tail_copy(h, q):
        return pltpu.make_async_copy(tail_hbm.at[:, :, pl.ds(q * piece, piece)], rec.at[h], tails.at[h - 1])

    for h in range(1, halos + 1):
        for q in range(h):
            @pl.when(me + h - n == q)
            def _():
                tail_copy(h, q).start()

    for copy in loads[5:]:
        copy.start()
    for copy in loads[:3]:
        copy.wait()
    lane = lax.broadcasted_iota(jnp.int32, (1, UNIT), 1)
    live = jnp.broadcast_to(count[...].reshape(1, 1), (1, UNIT))
    for q in range(2):
        spots = []
        for i in range(packs):
            if i < sides * comps:
                c = (q * sides + i // comps) * comps + i % comps
                row = padded(mov[c], UNIT)
                spots.append(jnp.where(lane < templates, jnp.where(c // comps < live, row, moves), 0))
            else:
                spots.append(jnp.where(lane < templates, jnp.broadcast_to(bank[...].reshape(1, 1), (1, UNIT)), 0))
        mine[q:q + 1] = lay(spots, templates)

    def meta_copy(step):
        return pltpu.make_async_remote_copy(
            src_ref=mine, dst_ref=meta.at[me], send_sem=meta_send, recv_sem=meta_recv,
            device_id={"reg": lax.rem(me + step, n)}, device_id_type=MESH)

    def halo_copy(h):
        return pltpu.make_async_remote_copy(
            src_ref=rec.at[0], dst_ref=rec.at[h], send_sem=halo_send.at[h - 1], recv_sem=halo_recv.at[h - 1],
            device_id={"reg": lax.rem(me + n - h, n)}, device_id_type=MESH)

    for copy in loads[3:5]:
        copy.wait()

    def choose(base):
        station = lax.broadcasted_iota(jnp.int32, (GROUP, regions), 0) + base
        for k in range(slots):
            here = jnp.broadcast_to(lists[k:k + 1], station.shape) == station
            member[k] = jnp.where(here, 1.0, 0.0)

    if groups == 1:
        choose(0)

    pl.semaphore_wait(barrier, n - 1)

    @pl.loop(1, n)
    def _(step):
        meta_copy(step).start()

    for h in range(1, halos + 1):
        @pl.when(me >= h)
        def _():
            halo_copy(h).start()

    meta[me] = mine[...]
    source = lax.broadcasted_iota(jnp.int32, (UNIT, UNIT), 0)
    target = lax.broadcasted_iota(jnp.int32, (UNIT, UNIT), 1)
    for i in range(packs):
        part = target // (UNIT // 2) if i // comps % 2 == 0 else 1 - target // (UNIT // 2)
        spread[i] = jnp.where(source == target % half + part * half + i * templates, 1.0, 0.0).astype(jnp.bfloat16)
    for i in range(quarters + 1):
        full = jnp.ones((UNIT, UNIT), jnp.float32)
        full = jnp.where(source >= target, full, 0.0) if i == 0 else full
        full = jnp.where(source < target, full, 0.0) if i == quarters else full
        band[i] = full.astype(jnp.bfloat16)
    for copy in loads[5:]:
        copy.wait()
    chunk = lax.broadcasted_iota(jnp.int32, (templates, UNIT), 1) // (UNIT // quarters)

    def reorder(e):
        now = [lib[j, e] for j in range(quarters)]
        bit = quarters // 2
        while bit:
            first = chunk // bit % 2 == 0
            reach = bit * (UNIT // quarters)
            then = list(now)
            for j in range(quarters):
                if not j & bit:
                    then[j] = jnp.where(first, now[j], pltpu.roll(now[j + bit], reach, 1))
                    then[j + bit] = jnp.where(first, pltpu.roll(now[j], UNIT - reach, 1), now[j + bit])
            now = then
            bit //= 2
        return now

    @pl.loop(0, banks // 2)
    def _(g):
        @pl.loop(0, channels, unroll=6)
        def _(c):
            at = g * (2 * channels) + c
            first, second = reorder(at), reorder(at + channels)
            for j in range(quarters):
                lib[j, at] = jnp.concatenate([first[j][:half], second[j][:half]], axis=0)
                lib[j, at + channels] = jnp.concatenate([first[j][half:], second[j][half:]], axis=0)

    everyone = meta.at[pl.ds(0, n - 1)]
    pltpu.make_async_copy(everyone, everyone, meta_recv).wait()

    for h in range(1, halos + 1):
        for q in range(h):
            @pl.when(me + h - n == q)
            def _():
                tail_copy(h, q).wait()

        @pl.when(me + h < n)
        def _():
            halo_copy(h).wait_recv()

    told = jnp.concatenate([meta[:, q, :] for q in range(2)], axis=0).astype(jnp.float32).astype(jnp.bfloat16)
    tiled = jnp.dot(told, jnp.concatenate([spread[i] for i in range(packs)], axis=1), preferred_element_type=jnp.float32)

    def facts(q, i):
        return tiled[q * regions:(q + 1) * regions, i * UNIT:(i + 1) * UNIT]

    wide = lax.broadcasted_iota(jnp.int32, (regions, UNIT), 1) // half % banks
    home = facts(0, sides * comps) == wide.astype(jnp.float32)

    def combine():
        left = lax.broadcasted_iota(jnp.int32, (GROUP, UNIT), 1) < UNIT // 2
        for p in range(slots // 2):
            many = []
            for k in (2 * p, 2 * p + 1):
                parts = []
                for c in range(comps):
                    q, side = divmod(k, sides)
                    shift = jnp.where(home, facts(q, side * comps + c), float(moves))
                    for m in range(moves):
                        parts.append(jnp.where(shift == m, 1.0, 0.0).astype(jnp.bfloat16))
                many.append(jnp.dot(member[k].astype(jnp.bfloat16), jnp.concatenate(parts, axis=1),
                                    preferred_element_type=jnp.float32))
            for i in range(comps * moves):
                even, odd = [one[:, i * UNIT:(i + 1) * UNIT] for one in many]
                tally[0, p, i] = jnp.where(left, even, odd)
                tally[1, p, i] = jnp.where(left, odd, even)
        own = (lax.broadcasted_iota(jnp.int32, (half, UNIT), 1) % half
               == lax.broadcasted_iota(jnp.int32, (half, UNIT), 0))

        for c in range(comps):
            for h in range(2):
                picks = [jnp.concatenate([
                    jnp.where(own, jnp.broadcast_to(tally[h, p, c * moves + m, s:s + 1], own.shape), 0.0)
                    for p in range(slots // 2)], axis=1) for s in range(GROUP) for m in range(moves)]
                weights = jnp.concatenate([
                    jnp.concatenate([lib[j, (2 * g + h) * channels + (2 * p + (side ^ h)) * comps + c]
                                     for j in range(quarters)], axis=1)
                    for p in range(slots // 2) for side in range(2) for g in range(banks // 2)], axis=0)
                total = jnp.dot(jnp.concatenate(picks, axis=0).astype(jnp.bfloat16), weights,
                                preferred_element_type=jnp.float32)
                for j in range(quarters):
                    for i in range(GROUP * moves):
                        to = i * templates + h * half
                        summed[c, j, to:to + half] = total[i * half:(i + 1) * half, j * UNIT:(j + 1) * UNIT]

    if groups == 1:
        combine()

    @pl.loop(0, stations, step=16)
    def _(s):
        s = pl.multiple_of(s, 16)
        squares = []
        for c in range(comps):
            x = jnp.concatenate([rec[p, c, pl.ds(s, 16)] for p in range(pieces)], axis=1).astype(jnp.float32)
            for k in range(16):
                moved = pltpu.roll(x, record - k, 1) if k else x
                for j in range(fans.shape[0]):
                    fans[j, pl.ds(k * pitch + c * stations + s, 16)] = moved[:, j * UNIT:(j + 1) * UNIT]
            square = x * x
            big = square.astype(jnp.bfloat16)
            squares.append((big, (square - big.astype(jnp.float32)).astype(jnp.bfloat16)))
        both = jnp.concatenate([part[i] for i in range(2) for part in squares], axis=0)
        energy = jnp.dot(
            jnp.concatenate([both[:, a * UNIT:(a + quarters + 1) * UNIT] for a in range(width // UNIT)], axis=0),
            jnp.concatenate([band[i] for i in range(quarters + 1)], axis=0), preferred_element_type=jnp.float32)
        half = 16 * comps
        levels = []
        for a in range(width // UNIT):
            total = energy[2 * a * half:(2 * a + 1) * half] + energy[(2 * a + 1) * half:(2 * a + 2) * half]
            levels.append(lax.rsqrt(total / taps + 1e-05) * scale)
        level = jnp.concatenate(levels + levels[:1], axis=1)
        for i in range(quarters):
            moved = pltpu.roll(level, i * (UNIT // quarters), 1) if i else level
            for c in range(comps):
                for b in range(gain.shape[1]):
                    gain[i, b, pl.ds(c * stations + s, 16)] = moved[c * 16:(c + 1) * 16, b * UNIT:(b + 1) * UNIT]

    across = piece // UNIT

    def correlate(c, s, within, totals):
        low = jnp.concatenate([fans[j, pl.ds(c * stations + s, 16, stride=pitch)]
                               for j in range(fans.shape[0])], axis=1).astype(jnp.bfloat16)
        high = pltpu.roll(low, record - 16, 1)

        def signal(first, count):
            rows = [part[:, (j + first) * UNIT:(j + first + count) * UNIT] for j in range(quarters) for part in (low, high)]
            return jnp.concatenate(rows + rows, axis=0)

        kernels = []
        for m in range(moves):
            at = pl.multiple_of((within * moves + m) * templates, templates)
            for i in range(quarters):
                whole = summed[c, i, pl.ds(at, templates)]
                big = whole.astype(jnp.bfloat16)
                small = (whole - big.astype(jnp.float32)).astype(jnp.bfloat16)
                kernels.append(jnp.concatenate([big, small], axis=1))
        for first in range(0, moves + across, across):
            count = min(across, moves + across - first)
            wanted = [(m, i, q) for m in range(moves) for i in range(quarters)
                      for q in [[b for b in range(first, first + count) if 0 <= b - m < across + (i > 0)]] if q]
            corr = jnp.dot(jnp.concatenate([kernels[m * quarters + i] for m, i, _ in wanted], axis=0),
                           signal(first, count), preferred_element_type=jnp.float32)
            for at, (m, i, q) in enumerate(wanted):
                for b in q:
                    one = corr[at * templates:(at + 1) * templates, (b - first) * UNIT:(b - first + 1) * UNIT]
                    one = one * gain[i, b, pl.ds(c * stations + s, 1)]
                    old = totals.get((i, b - m))
                    totals[i, b - m] = one if old is None else old + one

    partial[...] = jnp.zeros_like(partial)

    @pl.loop(0, groups)
    def _(g):
        if groups > 1:
            choose(g * GROUP)
            combine()

        @pl.loop(0, GROUP, step=SPAN)
        def _(within):
            totals = {}
            for i in range(SPAN):
                for c in range(comps):
                    correlate(c, g * GROUP + within + i, within + i, totals)
            for (i, q), total in totals.items():
                partial[i, q] += total

    result = None
    for i in range(quarters):
        whole = jnp.concatenate([partial[i, q] for q in range(across + 1)], axis=1)
        whole = pltpu.roll(whole, whole.shape[1] - i * (UNIT // quarters), 1) if i else whole
        result = whole if result is None else result + whole
    out_ref[...] = result[:, 0:piece]

    for h in range(1, halos + 1):
        @pl.when(me >= h)
        def _():
            halo_copy(h).wait_send()

    pltpu.make_async_copy(everyone, everyone, meta_send).wait()


def on_device(waveforms, tail, station_lists, station_count, bank_of_region, library, moveouts):
    n = lax.axis_size("reg")
    stations, comps, piece = waveforms.shape
    banks, templates, channels, taps = library.shape
    regions, slots = station_lists.shape
    scale = 1.0 / math.sqrt(comps * slots * regions)
    pieces = 1 + tail.shape[2] // piece
    record = pieces * piece
    moves = (record - piece - taps) // UNIT + 1
    width = record - taps
    packs = UNIT // templates
    bank_rows = jnp.transpose(library, (0, 2, 1, 3)).reshape(banks * channels, templates, taps)
    anywhere = pl.BlockSpec(memory_space=pltpu.HBM)
    return pl.pallas_call(
        functools.partial(kernel, n, taps, scale),
        out_shape=jax.ShapeDtypeStruct((templates, piece), jnp.float32),
        in_specs=[anywhere] * 7,
        out_specs=pl.BlockSpec(memory_space=pltpu.VMEM),
        scratch_shapes=[
            pltpu.VMEM((pieces, comps, stations, piece), jnp.bfloat16),
            pltpu.VMEM((slots, regions), jnp.int32),
            pltpu.VMEM((1,), jnp.int32),
            pltpu.VMEM((1,), jnp.int32),
            pltpu.VMEM((taps // UNIT, banks * channels, templates, UNIT), library.dtype),
            pltpu.VMEM((channels, 1, templates), jnp.int32),
            pltpu.VMEM((2, UNIT), jnp.int32),
            pltpu.VMEM((n, 2, UNIT), jnp.int32),
            pltpu.VMEM((packs, UNIT, UNIT), jnp.bfloat16),
            pltpu.VMEM((taps // UNIT + 1, UNIT, UNIT), jnp.bfloat16),
            pltpu.VMEM((slots, GROUP, regions), jnp.float32),
            pltpu.VMEM((2, slots // 2, comps * moves, GROUP, UNIT), jnp.float32),
            pltpu.VMEM((comps, taps // UNIT, GROUP * moves * templates, UNIT), jnp.float32),
            pltpu.VMEM((record // UNIT, 16 * (comps * stations + 1), UNIT), jnp.float32),
            pltpu.VMEM((taps // UNIT, width // UNIT + 1, comps * stations, UNIT), jnp.float32),
            pltpu.VMEM((taps // UNIT, piece // UNIT + 1, templates, UNIT), jnp.float32),
            pltpu.SemaphoreType.DMA((5 + taps // UNIT,)),
            pltpu.SemaphoreType.DMA((pieces - 1,)),
            pltpu.SemaphoreType.DMA((pieces - 1,)),
            pltpu.SemaphoreType.DMA((pieces - 1,)),
            pltpu.SemaphoreType.DMA,
            pltpu.SemaphoreType.DMA,
        ],
        compiler_params=pltpu.CompilerParams(collective_id=0, has_side_effects=True,
                                             vmem_limit_bytes=60 << 20),
        name="matched",
    )(jnp.transpose(waveforms, (1, 0, 2)), jnp.transpose(tail, (1, 0, 2)), station_lists.T,
      station_count, bank_of_region, bank_rows, jnp.transpose(moveouts, (2, 0, 1)))


def solution(mesh):
    return jax.shard_map(
        on_device,
        mesh=mesh,
        in_specs=(
            P("grp", None, "reg"),
            P("grp", None, None),
            P("grp", None),
            P(("grp", "reg")),
            P(("grp", "reg")),
            P(),
            P(("grp", "reg"), None, None),
        ),
        out_specs=P("grp", "reg"),
        check_vma=False,
    )
```

```python
import functools
import math

import jax
import jax.numpy as jnp
from jax import lax
from jax.experimental import pallas as pl
from jax.experimental.pallas import tpu as pltpu
from jax.sharding import PartitionSpec as P

UNIT = 128
GROUP = 16
SPAN = 8
MESH = pl.DeviceIdType.MESH


def lay(blocks, width):
    if width % UNIT == 0:
        return jnp.concatenate(blocks, axis=1)
    per = UNIT // width
    tiles = []
    for start in range(0, len(blocks), per):
        tile = blocks[start]
        for i, block in enumerate(blocks[start + 1:start + per]):
            tile = tile + pltpu.roll(block, (i + 1) * width, 1)
        tiles.append(tile)
    return jnp.concatenate(tiles, axis=1)


def padded(x, lanes):
    if x.shape[1] % lanes == 0:
        return x
    return jnp.concatenate([x, jnp.zeros((x.shape[0], lanes - x.shape[1] % lanes), x.dtype)], axis=1)


def kernel(n, taps, scale, wave_hbm, tail_hbm, lists_hbm, count_hbm, bank_hbm, lib_hbm, mov_hbm, out_ref,
           rec, lists, count, bank, lib, mov, mine, meta, spread, band, member, tally, summed, fans, gain, partial,
           local, tails, halo_send, halo_recv, meta_send, meta_recv):
    me = lax.axis_index("reg")
    pieces, comps, stations, piece = rec.shape
    halos = pieces - 1
    record = pieces * piece
    channels, _, templates = mov.shape
    slots, regions = lists.shape
    quarters = taps // UNIT
    banks = lib.shape[1] // channels
    moves = (record - piece - taps) // UNIT + 1
    width = piece + (moves - 1) * UNIT
    pitch = comps * stations + 1
    packs = UNIT // templates
    sides = slots // 2
    half = templates // 2
    groups = stations // GROUP

    barrier = pltpu.get_barrier_semaphore()
    loads = [pltpu.make_async_copy(src, dst, local.at[i]) for i, (src, dst) in enumerate(
        [(mov_hbm, mov), (count_hbm, count), (bank_hbm, bank), (lists_hbm, lists), (wave_hbm, rec.at[0])]
        + [(lib_hbm.at[:, :, j * UNIT:(j + 1) * UNIT], lib.at[j]) for j in range(quarters)])]

    for copy in loads[:5]:
        copy.start()

    @pl.loop(1, n)
    def _(step):
        pl.semaphore_signal(barrier, inc=1, device_id={"reg": lax.rem(me + step, n)}, device_id_type=MESH)

    def tail_copy(h, q):
        return pltpu.make_async_copy(tail_hbm.at[:, :, pl.ds(q * piece, piece)], rec.at[h], tails.at[h - 1])

    for h in range(1, halos + 1):
        for q in range(h):
            @pl.when(me + h - n == q)
            def _():
                tail_copy(h, q).start()

    for copy in loads[5:]:
        copy.start()
    for copy in loads[:3]:
        copy.wait()
    lane = lax.broadcasted_iota(jnp.int32, (1, UNIT), 1)
    live = jnp.broadcast_to(count[...].reshape(1, 1), (1, UNIT))
    for q in range(2):
        spots = []
        for i in range(packs):
            if i < sides * comps:
                c = (q * sides + i // comps) * comps + i % comps
                row = padded(mov[c], UNIT)
                spots.append(jnp.where(lane < templates, jnp.where(c // comps < live, row, moves), 0))
            else:
                spots.append(jnp.where(lane < templates, jnp.broadcast_to(bank[...].reshape(1, 1), (1, UNIT)), 0))
        mine[q:q + 1] = lay(spots, templates)

    def meta_copy(step):
        return pltpu.make_async_remote_copy(
            src_ref=mine, dst_ref=meta.at[me], send_sem=meta_send, recv_sem=meta_recv,
            device_id={"reg": lax.rem(me + step, n)}, device_id_type=MESH)

    def halo_copy(h):
        return pltpu.make_async_remote_copy(
            src_ref=rec.at[0], dst_ref=rec.at[h], send_sem=halo_send.at[h - 1], recv_sem=halo_recv.at[h - 1],
            device_id={"reg": lax.rem(me + n - h, n)}, device_id_type=MESH)

    for copy in loads[3:5]:
        copy.wait()

    def choose(base):
        station = lax.broadcasted_iota(jnp.int32, (GROUP, regions), 0) + base
        for k in range(slots):
            here = jnp.broadcast_to(lists[k:k + 1], station.shape) == station
            member[k] = jnp.where(here, 1.0, 0.0)

    if groups == 1:
        choose(0)

    pl.semaphore_wait(barrier, n - 1)

    @pl.loop(1, n)
    def _(step):
        meta_copy(step).start()

    for h in range(1, halos + 1):
        @pl.when(me >= h)
        def _():
            halo_copy(h).start()

    meta[me] = mine[...]
    source = lax.broadcasted_iota(jnp.int32, (UNIT, UNIT), 0)
    target = lax.broadcasted_iota(jnp.int32, (UNIT, UNIT), 1)
    for i in range(packs):
        part = target // (UNIT // 2) if i // comps % 2 == 0 else 1 - target // (UNIT // 2)
        spread[i] = jnp.where(source == target % half + part * half + i * templates, 1.0, 0.0).astype(jnp.bfloat16)
    for i in range(quarters + 1):
        full = jnp.ones((UNIT, UNIT), jnp.float32)
        full = jnp.where(source >= target, full, 0.0) if i == 0 else full
        full = jnp.where(source < target, full, 0.0) if i == quarters else full
        band[i] = full.astype(jnp.bfloat16)
    for copy in loads[5:]:
        copy.wait()
    chunk = lax.broadcasted_iota(jnp.int32, (templates, UNIT), 1) // (UNIT // quarters)

    def reorder(e):
        now = [lib[j, e] for j in range(quarters)]
        bit = quarters // 2
        while bit:
            first = chunk // bit % 2 == 0
            reach = bit * (UNIT // quarters)
            then = list(now)
            for j in range(quarters):
                if not j & bit:
                    then[j] = jnp.where(first, now[j], pltpu.roll(now[j + bit], reach, 1))
                    then[j + bit] = jnp.where(first, pltpu.roll(now[j], UNIT - reach, 1), now[j + bit])
            now = then
            bit //= 2
        return now

    @pl.loop(0, banks // 2)
    def _(g):
        @pl.loop(0, channels, unroll=6)
        def _(c):
            at = g * (2 * channels) + c
            first, second = reorder(at), reorder(at + channels)
            for j in range(quarters):
                lib[j, at] = jnp.concatenate([first[j][:half], second[j][:half]], axis=0)
                lib[j, at + channels] = jnp.concatenate([first[j][half:], second[j][half:]], axis=0)

    everyone = meta.at[pl.ds(0, n - 1)]
    pltpu.make_async_copy(everyone, everyone, meta_recv).wait()

    for h in range(1, halos + 1):
        for q in range(h):
            @pl.when(me + h - n == q)
            def _():
                tail_copy(h, q).wait()

        @pl.when(me + h < n)
        def _():
            halo_copy(h).wait_recv()

    told = jnp.concatenate([meta[:, q, :] for q in range(2)], axis=0).astype(jnp.float32).astype(jnp.bfloat16)
    tiled = jnp.dot(told, jnp.concatenate([spread[i] for i in range(packs)], axis=1), preferred_element_type=jnp.float32)

    def facts(q, i):
        return tiled[q * regions:(q + 1) * regions, i * UNIT:(i + 1) * UNIT]

    wide = lax.broadcasted_iota(jnp.int32, (regions, UNIT), 1) // half % banks
    home = facts(0, sides * comps) == wide.astype(jnp.float32)

    def unfold(s):
        s = s if stations == 16 else pl.multiple_of(s, 16)
        squares = []
        for c in range(comps):
            x = jnp.concatenate([rec[p, c, pl.ds(s, 16)] for p in range(pieces)], axis=1).astype(jnp.float32)
            for k in range(16):
                moved = pltpu.roll(x, record - k, 1) if k else x
                for j in range(fans.shape[0]):
                    fans[j, pl.ds(k * pitch + c * stations + s, 16)] = moved[:, j * UNIT:(j + 1) * UNIT]
            square = x * x
            big = square.astype(jnp.bfloat16)
            squares.append((big, (square - big.astype(jnp.float32)).astype(jnp.bfloat16)))
        both = jnp.concatenate([part[i] for i in range(2) for part in squares], axis=0)
        energy = jnp.dot(
            jnp.concatenate([both[:, a * UNIT:(a + quarters + 1) * UNIT] for a in range(width // UNIT)], axis=0),
            jnp.concatenate([band[i] for i in range(quarters + 1)], axis=0), preferred_element_type=jnp.float32)
        half = 16 * comps
        levels = []
        for a in range(width // UNIT):
            total = energy[2 * a * half:(2 * a + 1) * half] + energy[(2 * a + 1) * half:(2 * a + 2) * half]
            levels.append(lax.rsqrt(total / taps + 1e-05) * scale)
        level = jnp.concatenate(levels + levels[:1], axis=1)
        for i in range(quarters):
            moved = pltpu.roll(level, i * (UNIT // quarters), 1) if i else level
            for c in range(comps):
                for b in range(gain.shape[1]):
                    gain[i, b, pl.ds(c * stations + s, 16)] = moved[c * 16:(c + 1) * 16, b * UNIT:(b + 1) * UNIT]

    if stations == 16:
        unfold(0)
    else:
        pl.loop(0, stations, step=16)(unfold)

    def combine():
        left = lax.broadcasted_iota(jnp.int32, (GROUP, UNIT), 1) < UNIT // 2
        for p in range(slots // 2):
            many = []
            for k in (2 * p, 2 * p + 1):
                parts = []
                for c in range(comps):
                    q, side = divmod(k, sides)
                    shift = jnp.where(home, facts(q, side * comps + c), float(moves))
                    for m in range(moves):
                        parts.append(jnp.where(shift == m, 1.0, 0.0).astype(jnp.bfloat16))
                many.append(jnp.dot(member[k].astype(jnp.bfloat16), jnp.concatenate(parts, axis=1),
                                    preferred_element_type=jnp.float32))
            for i in range(comps * moves):
                even, odd = [one[:, i * UNIT:(i + 1) * UNIT] for one in many]
                tally[0, p, i] = jnp.where(left, even, odd)
                tally[1, p, i] = jnp.where(left, odd, even)
        own = (lax.broadcasted_iota(jnp.int32, (half, UNIT), 1) % half
               == lax.broadcasted_iota(jnp.int32, (half, UNIT), 0))

        for c in range(comps):
            for h in range(2):
                picks = [jnp.concatenate([
                    jnp.where(own, jnp.broadcast_to(tally[h, p, c * moves + m, s:s + 1], own.shape), 0.0)
                    for p in range(slots // 2)], axis=1) for s in range(GROUP) for m in range(moves)]
                weights = jnp.concatenate([
                    jnp.concatenate([lib[j, (2 * g + h) * channels + (2 * p + (side ^ h)) * comps + c]
                                     for j in range(quarters)], axis=1)
                    for p in range(slots // 2) for side in range(2) for g in range(banks // 2)], axis=0)
                total = jnp.dot(jnp.concatenate(picks, axis=0).astype(jnp.bfloat16), weights,
                                preferred_element_type=jnp.float32)
                for j in range(quarters):
                    for i in range(GROUP * moves):
                        to = i * templates + h * half
                        summed[c, j, to:to + half] = total[i * half:(i + 1) * half, j * UNIT:(j + 1) * UNIT]

    if groups == 1:
        combine()

    across = piece // UNIT

    def correlate(c, s, within, totals):
        low = jnp.concatenate([fans[j, pl.ds(c * stations + s, 16, stride=pitch)]
                               for j in range(fans.shape[0])], axis=1).astype(jnp.bfloat16)
        high = pltpu.roll(low, record - 16, 1)

        def signal(first, count):
            rows = [part[:, (j + first) * UNIT:(j + first + count) * UNIT] for j in range(quarters) for part in (low, high)]
            return jnp.concatenate(rows + rows, axis=0)

        kernels = []
        for m in range(moves):
            at = pl.multiple_of((within * moves + m) * templates, templates)
            for i in range(quarters):
                whole = summed[c, i, pl.ds(at, templates)]
                big = whole.astype(jnp.bfloat16)
                small = (whole - big.astype(jnp.float32)).astype(jnp.bfloat16)
                kernels.append(jnp.concatenate([big, small], axis=1))
        for first in range(0, moves + across, across):
            count = min(across, moves + across - first)
            wanted = [(m, i, q) for m in range(moves) for i in range(quarters)
                      for q in [[b for b in range(first, first + count) if 0 <= b - m < across + (i > 0)]] if q]
            corr = jnp.dot(jnp.concatenate([kernels[m * quarters + i] for m, i, _ in wanted], axis=0),
                           signal(first, count), preferred_element_type=jnp.float32)
            for at, (m, i, q) in enumerate(wanted):
                for b in q:
                    one = corr[at * templates:(at + 1) * templates, (b - first) * UNIT:(b - first + 1) * UNIT]
                    one = one * gain[i, b, pl.ds(c * stations + s, 1)]
                    old = totals.get((i, b - m))
                    totals[i, b - m] = one if old is None else old + one

    partial[...] = jnp.zeros_like(partial)

    @pl.loop(0, groups)
    def _(g):
        if groups > 1:
            choose(g * GROUP)
            combine()

        @pl.loop(0, GROUP, step=SPAN)
        def _(within):
            totals = {}
            for i in range(SPAN):
                for c in range(comps):
                    correlate(c, g * GROUP + within + i, within + i, totals)
            for (i, q), total in totals.items():
                partial[i, q] += total

    result = None
    for i in range(quarters):
        whole = jnp.concatenate([partial[i, q] for q in range(across + 1)], axis=1)
        whole = pltpu.roll(whole, whole.shape[1] - i * (UNIT // quarters), 1) if i else whole
        result = whole if result is None else result + whole
    out_ref[...] = result[:, 0:piece]

    for h in range(1, halos + 1):
        @pl.when(me >= h)
        def _():
            halo_copy(h).wait_send()

    pltpu.make_async_copy(everyone, everyone, meta_send).wait()


def on_device(waveforms, tail, station_lists, station_count, bank_of_region, library, moveouts):
    n = lax.axis_size("reg")
    stations, comps, piece = waveforms.shape
    banks, templates, channels, taps = library.shape
    regions, slots = station_lists.shape
    scale = 1.0 / math.sqrt(comps * slots * regions)
    pieces = 1 + tail.shape[2] // piece
    record = pieces * piece
    moves = (record - piece - taps) // UNIT + 1
    width = record - taps
    packs = UNIT // templates
    bank_rows = jnp.transpose(library, (0, 2, 1, 3)).reshape(banks * channels, templates, taps)
    anywhere = pl.BlockSpec(memory_space=pltpu.HBM)
    return pl.pallas_call(
        functools.partial(kernel, n, taps, scale),
        out_shape=jax.ShapeDtypeStruct((templates, piece), jnp.float32),
        in_specs=[anywhere] * 7,
        out_specs=pl.BlockSpec(memory_space=pltpu.VMEM),
        scratch_shapes=[
            pltpu.VMEM((pieces, comps, stations, piece), jnp.bfloat16),
            pltpu.VMEM((slots, regions), jnp.int32),
            pltpu.VMEM((1,), jnp.int32),
            pltpu.VMEM((1,), jnp.int32),
            pltpu.VMEM((taps // UNIT, banks * channels, templates, UNIT), library.dtype),
            pltpu.VMEM((channels, 1, templates), jnp.int32),
            pltpu.VMEM((2, UNIT), jnp.int32),
            pltpu.VMEM((n, 2, UNIT), jnp.int32),
            pltpu.VMEM((packs, UNIT, UNIT), jnp.bfloat16),
            pltpu.VMEM((taps // UNIT + 1, UNIT, UNIT), jnp.bfloat16),
            pltpu.VMEM((slots, GROUP, regions), jnp.float32),
            pltpu.VMEM((2, slots // 2, comps * moves, GROUP, UNIT), jnp.float32),
            pltpu.VMEM((comps, taps // UNIT, GROUP * moves * templates, UNIT), jnp.float32),
            pltpu.VMEM((record // UNIT, 16 * (comps * stations + 1), UNIT), jnp.float32),
            pltpu.VMEM((taps // UNIT, width // UNIT + 1, comps * stations, UNIT), jnp.float32),
            pltpu.VMEM((taps // UNIT, piece // UNIT + 1, templates, UNIT), jnp.float32),
            pltpu.SemaphoreType.DMA((5 + taps // UNIT,)),
            pltpu.SemaphoreType.DMA((pieces - 1,)),
            pltpu.SemaphoreType.DMA((pieces - 1,)),
            pltpu.SemaphoreType.DMA((pieces - 1,)),
            pltpu.SemaphoreType.DMA,
            pltpu.SemaphoreType.DMA,
        ],
        compiler_params=pltpu.CompilerParams(collective_id=0, has_side_effects=True,
                                             vmem_limit_bytes=50 << 20),
        name="matched",
    )(*[x if x.size == 1 else pltpu.with_memory_space_constraint(x, pltpu.HBM) for x in (
        jnp.transpose(waveforms, (1, 0, 2)), jnp.transpose(tail, (1, 0, 2)), station_lists.T,
        station_count, bank_of_region, bank_rows, jnp.transpose(moveouts, (2, 0, 1)))])


def solution(mesh):
    return jax.shard_map(
        on_device,
        mesh=mesh,
        in_specs=(
            P("grp", None, "reg"),
            P("grp", None, None),
            P("grp", None),
            P(("grp", "reg")),
            P(("grp", "reg")),
            P(),
            P(("grp", "reg"), None, None),
        ),
        out_specs=P("grp", "reg"),
        check_vma=False,
    )
```

```python
import functools
import math

import jax
import jax.numpy as jnp
from jax import lax
from jax.experimental import pallas as pl
from jax.experimental.pallas import tpu as pltpu
from jax.sharding import PartitionSpec as P

UNIT = 128
GROUP = 16
SPAN = 8
MESH = pl.DeviceIdType.MESH


def lay(blocks, width):
    if width % UNIT == 0:
        return jnp.concatenate(blocks, axis=1)
    per = UNIT // width
    tiles = []
    for start in range(0, len(blocks), per):
        tile = blocks[start]
        for i, block in enumerate(blocks[start + 1:start + per]):
            tile = tile + pltpu.roll(block, (i + 1) * width, 1)
        tiles.append(tile)
    return jnp.concatenate(tiles, axis=1)


def padded(x, lanes):
    if x.shape[1] % lanes == 0:
        return x
    return jnp.concatenate([x, jnp.zeros((x.shape[0], lanes - x.shape[1] % lanes), x.dtype)], axis=1)


def kernel(n, taps, scale, wave_hbm, tail_hbm, lists_hbm, count_hbm, bank_hbm, lib_hbm, mov_hbm, out_ref,
           rec, lists, count, bank, lib, mov, mine, meta, spread, band, member, tally, summed, fans, gain, partial,
           local, tails, halo_send, halo_recv, meta_send, meta_recv):
    me = lax.axis_index("reg")
    pieces, comps, stations, piece = rec.shape
    halos = pieces - 1
    record = pieces * piece
    channels, _, templates = mov.shape
    slots, regions = lists.shape
    quarters = taps // UNIT
    banks = lib.shape[1] // channels
    moves = (record - piece - taps) // UNIT + 1
    width = piece + (moves - 1) * UNIT
    pitch = comps * stations + 1
    packs = UNIT // templates
    sides = slots // 2
    half = templates // 2
    groups = stations // GROUP

    barrier = pltpu.get_barrier_semaphore()
    loads = [pltpu.make_async_copy(src, dst, local.at[i]) for i, (src, dst) in enumerate(
        [(mov_hbm, mov), (count_hbm, count), (bank_hbm, bank), (lists_hbm, lists), (wave_hbm, rec.at[0])]
        + [(lib_hbm.at[:, :, j * UNIT:(j + 1) * UNIT], lib.at[j]) for j in range(quarters)])]

    for copy in loads[:5]:
        copy.start()

    @pl.loop(1, n)
    def _(step):
        pl.semaphore_signal(barrier, inc=1, device_id={"reg": lax.rem(me + step, n)}, device_id_type=MESH)

    def tail_copy(h, q):
        return pltpu.make_async_copy(tail_hbm.at[:, :, pl.ds(q * piece, piece)], rec.at[h], tails.at[h - 1])

    for h in range(1, halos + 1):
        for q in range(h):
            @pl.when(me + h - n == q)
            def _():
                tail_copy(h, q).start()

    for copy in loads[5:]:
        copy.start()
    for copy in loads[:3]:
        copy.wait()
    lane = lax.broadcasted_iota(jnp.int32, (1, UNIT), 1)
    live = jnp.broadcast_to(count[...].reshape(1, 1), (1, UNIT))
    for q in range(2):
        spots = []
        for i in range(packs):
            if i < sides * comps:
                c = (q * sides + i // comps) * comps + i % comps
                row = padded(mov[c], UNIT)
                spots.append(jnp.where(lane < templates, jnp.where(c // comps < live, row, moves), 0))
            else:
                spots.append(jnp.where(lane < templates, jnp.broadcast_to(bank[...].reshape(1, 1), (1, UNIT)), 0))
        mine[q:q + 1] = lay(spots, templates)

    def meta_copy(step):
        return pltpu.make_async_remote_copy(
            src_ref=mine, dst_ref=meta.at[me], send_sem=meta_send, recv_sem=meta_recv,
            device_id={"reg": lax.rem(me + step, n)}, device_id_type=MESH)

    def halo_copy(h):
        return pltpu.make_async_remote_copy(
            src_ref=rec.at[0], dst_ref=rec.at[h], send_sem=halo_send.at[h - 1], recv_sem=halo_recv.at[h - 1],
            device_id={"reg": lax.rem(me + n - h, n)}, device_id_type=MESH)

    for copy in loads[3:5]:
        copy.wait()

    def choose(base):
        station = lax.broadcasted_iota(jnp.int32, (GROUP, regions), 0) + base
        for k in range(slots):
            here = jnp.broadcast_to(lists[k:k + 1], station.shape) == station
            member[k] = jnp.where(here, 1.0, 0.0)

    if groups == 1:
        choose(0)

    pl.semaphore_wait(barrier, n - 1)

    @pl.loop(1, n)
    def _(step):
        meta_copy(step).start()

    for h in range(1, halos + 1):
        @pl.when(me >= h)
        def _():
            halo_copy(h).start()

    meta[me] = mine[...]
    source = lax.broadcasted_iota(jnp.int32, (UNIT, UNIT), 0)
    target = lax.broadcasted_iota(jnp.int32, (UNIT, UNIT), 1)
    for i in range(packs):
        part = target // (UNIT // 2) if i // comps % 2 == 0 else 1 - target // (UNIT // 2)
        spread[i] = jnp.where(source == target % half + part * half + i * templates, 1.0, 0.0).astype(jnp.bfloat16)
    for i in range(quarters + 1):
        full = jnp.ones((UNIT, UNIT), jnp.float32)
        full = jnp.where(source >= target, full, 0.0) if i == 0 else full
        full = jnp.where(source < target, full, 0.0) if i == quarters else full
        band[i] = full.astype(jnp.bfloat16)
    for copy in loads[5:]:
        copy.wait()
    chunk = lax.broadcasted_iota(jnp.int32, (templates, UNIT), 1) // (UNIT // quarters)

    def reorder(e):
        now = [lib[j, e] for j in range(quarters)]
        bit = quarters // 2
        while bit:
            first = chunk // bit % 2 == 0
            reach = bit * (UNIT // quarters)
            then = list(now)
            for j in range(quarters):
                if not j & bit:
                    then[j] = jnp.where(first, now[j], pltpu.roll(now[j + bit], reach, 1))
                    then[j + bit] = jnp.where(first, pltpu.roll(now[j], UNIT - reach, 1), now[j + bit])
            now = then
            bit //= 2
        return now

    @pl.loop(0, banks // 2)
    def _(g):
        @pl.loop(0, channels, unroll=6)
        def _(c):
            at = g * (2 * channels) + c
            first, second = reorder(at), reorder(at + channels)
            for j in range(quarters):
                lib[j, at] = jnp.concatenate([first[j][:half], second[j][:half]], axis=0)
                lib[j, at + channels] = jnp.concatenate([first[j][half:], second[j][half:]], axis=0)

    everyone = meta.at[pl.ds(0, n - 1)]
    pltpu.make_async_copy(everyone, everyone, meta_recv).wait()

    for h in range(1, halos + 1):
        for q in range(h):
            @pl.when(me + h - n == q)
            def _():
                tail_copy(h, q).wait()

        @pl.when(me + h < n)
        def _():
            halo_copy(h).wait_recv()

    told = jnp.concatenate([meta[:, q, :] for q in range(2)], axis=0).astype(jnp.float32).astype(jnp.bfloat16)
    tiled = jnp.dot(told, jnp.concatenate([spread[i] for i in range(packs)], axis=1), preferred_element_type=jnp.float32)

    def facts(q, i):
        return tiled[q * regions:(q + 1) * regions, i * UNIT:(i + 1) * UNIT]

    wide = lax.broadcasted_iota(jnp.int32, (regions, UNIT), 1) // half % banks
    home = facts(0, sides * comps) == wide.astype(jnp.float32)

    def unfold(s):
        s = s if stations == 16 else pl.multiple_of(s, 16)
        squares = []
        for c in range(comps):
            x = jnp.concatenate([rec[p, c, pl.ds(s, 16)] for p in range(pieces)], axis=1).astype(jnp.float32)
            for k in range(16):
                moved = pltpu.roll(x, record - k, 1) if k else x
                for j in range(fans.shape[0]):
                    fans[j, pl.ds(k * pitch + c * stations + s, 16)] = moved[:, j * UNIT:(j + 1) * UNIT]
            square = x * x
            big = square.astype(jnp.bfloat16)
            squares.append((big, (square - big.astype(jnp.float32)).astype(jnp.bfloat16)))
        both = jnp.concatenate([part[i] for i in range(2) for part in squares], axis=0)
        energy = jnp.dot(
            jnp.concatenate([both[:, a * UNIT:(a + quarters + 1) * UNIT] for a in range(width // UNIT)], axis=0),
            jnp.concatenate([band[i] for i in range(quarters + 1)], axis=0), preferred_element_type=jnp.float32)
        half = 16 * comps
        levels = []
        for a in range(width // UNIT):
            total = energy[2 * a * half:(2 * a + 1) * half] + energy[(2 * a + 1) * half:(2 * a + 2) * half]
            levels.append(lax.rsqrt(total / taps + 1e-05) * scale)
        level = jnp.concatenate(levels + levels[:1], axis=1)
        for i in range(quarters):
            moved = pltpu.roll(level, i * (UNIT // quarters), 1) if i else level
            for c in range(comps):
                for b in range(gain.shape[1]):
                    gain[i, b, pl.ds(c * stations + s, 16)] = moved[c * 16:(c + 1) * 16, b * UNIT:(b + 1) * UNIT]

    if stations == 16:
        unfold(0)
    else:
        pl.loop(0, stations, step=16)(unfold)

    def combine():
        left = lax.broadcasted_iota(jnp.int32, (GROUP, UNIT), 1) < UNIT // 2
        for p in range(slots // 2):
            many = []
            for k in (2 * p, 2 * p + 1):
                parts = []
                for c in range(comps):
                    q, side = divmod(k, sides)
                    shift = jnp.where(home, facts(q, side * comps + c), float(moves))
                    for m in range(moves):
                        parts.append(jnp.where(shift == m, 1.0, 0.0).astype(jnp.bfloat16))
                many.append(jnp.dot(member[k].astype(jnp.bfloat16), jnp.concatenate(parts, axis=1),
                                    preferred_element_type=jnp.float32))
            for i in range(comps * moves):
                even, odd = [one[:, i * UNIT:(i + 1) * UNIT] for one in many]
                tally[0, p, i] = jnp.where(left, even, odd)
                tally[1, p, i] = jnp.where(left, odd, even)
        own = (lax.broadcasted_iota(jnp.int32, (half, UNIT), 1) % half
               == lax.broadcasted_iota(jnp.int32, (half, UNIT), 0))

        for c in range(comps):
            for h in range(2):
                picks = [jnp.concatenate([
                    jnp.where(own, jnp.broadcast_to(tally[h, p, c * moves + m, s:s + 1], own.shape), 0.0)
                    for p in range(slots // 2)], axis=1) for s in range(GROUP) for m in range(moves)]
                weights = jnp.concatenate([
                    jnp.concatenate([lib[j, (2 * g + h) * channels + (2 * p + (side ^ h)) * comps + c]
                                     for j in range(quarters)], axis=1)
                    for p in range(slots // 2) for side in range(2) for g in range(banks // 2)], axis=0)
                total = jnp.dot(jnp.concatenate(picks, axis=0).astype(jnp.bfloat16), weights,
                                preferred_element_type=jnp.float32)
                for j in range(quarters):
                    for i in range(GROUP * moves):
                        to = i * templates + h * half
                        summed[c, j, to:to + half] = total[i * half:(i + 1) * half, j * UNIT:(j + 1) * UNIT]

    if groups == 1:
        combine()

    across = piece // UNIT

    def correlate(c, s, within, totals):
        low = jnp.concatenate([fans[j, pl.ds(c * stations + s, 16, stride=pitch)]
                               for j in range(fans.shape[0])], axis=1).astype(jnp.bfloat16)
        high = pltpu.roll(low, record - 16, 1)

        def signal(first, count):
            rows = [part[:, (j + first) * UNIT:(j + first + count) * UNIT] for j in range(quarters) for part in (low, high)]
            return jnp.concatenate(rows + rows, axis=0)

        kernels = []
        for m in range(moves):
            at = pl.multiple_of((within * moves + m) * templates, templates)
            for i in range(quarters):
                whole = summed[c, i, pl.ds(at, templates)]
                big = whole.astype(jnp.bfloat16)
                small = (whole - big.astype(jnp.float32)).astype(jnp.bfloat16)
                kernels.append(jnp.concatenate([big, small], axis=1))
        for first, count in ((0, 2), (2, 1), (3, 2)):
            wanted = [(m, i, q) for m in range(moves) for i in range(quarters)
                      for q in [[b for b in range(first, first + count) if 0 <= b - m < across + (i > 0)]] if q]
            corr = jnp.dot(jnp.concatenate([kernels[m * quarters + i] for m, i, _ in wanted], axis=0),
                           signal(first, count), preferred_element_type=jnp.float32)
            for at, (m, i, q) in enumerate(wanted):
                for b in q:
                    one = corr[at * templates:(at + 1) * templates, (b - first) * UNIT:(b - first + 1) * UNIT]
                    one = one * gain[i, b, pl.ds(c * stations + s, 1)]
                    old = totals.get((i, b - m))
                    totals[i, b - m] = one if old is None else old + one

    partial[...] = jnp.zeros_like(partial)

    @pl.loop(0, groups)
    def _(g):
        if groups > 1:
            choose(g * GROUP)
            combine()

        @pl.loop(0, GROUP, step=SPAN)
        def _(within):
            totals = {}
            for i in range(SPAN):
                for c in range(comps):
                    correlate(c, g * GROUP + within + i, within + i, totals)
            for (i, q), total in totals.items():
                partial[i, q] += total

    result = None
    for i in range(quarters):
        whole = jnp.concatenate([partial[i, q] for q in range(across + 1)], axis=1)
        whole = pltpu.roll(whole, whole.shape[1] - i * (UNIT // quarters), 1) if i else whole
        result = whole if result is None else result + whole
    out_ref[...] = result[:, 0:piece]

    for h in range(1, halos + 1):
        @pl.when(me >= h)
        def _():
            halo_copy(h).wait_send()

    pltpu.make_async_copy(everyone, everyone, meta_send).wait()


def on_device(waveforms, tail, station_lists, station_count, bank_of_region, library, moveouts):
    n = lax.axis_size("reg")
    stations, comps, piece = waveforms.shape
    banks, templates, channels, taps = library.shape
    regions, slots = station_lists.shape
    scale = 1.0 / math.sqrt(comps * slots * regions)
    pieces = 1 + tail.shape[2] // piece
    record = pieces * piece
    moves = (record - piece - taps) // UNIT + 1
    width = record - taps
    packs = UNIT // templates
    bank_rows = jnp.transpose(library, (0, 2, 1, 3)).reshape(banks * channels, templates, taps)
    anywhere = pl.BlockSpec(memory_space=pltpu.HBM)
    return pl.pallas_call(
        functools.partial(kernel, n, taps, scale),
        out_shape=jax.ShapeDtypeStruct((templates, piece), jnp.float32),
        in_specs=[anywhere] * 7,
        out_specs=pl.BlockSpec(memory_space=pltpu.VMEM),
        scratch_shapes=[
            pltpu.VMEM((pieces, comps, stations, piece), jnp.bfloat16),
            pltpu.VMEM((slots, regions), jnp.int32),
            pltpu.VMEM((1,), jnp.int32),
            pltpu.VMEM((1,), jnp.int32),
            pltpu.VMEM((taps // UNIT, banks * channels, templates, UNIT), library.dtype),
            pltpu.VMEM((channels, 1, templates), jnp.int32),
            pltpu.VMEM((2, UNIT), jnp.int32),
            pltpu.VMEM((n, 2, UNIT), jnp.int32),
            pltpu.VMEM((packs, UNIT, UNIT), jnp.bfloat16),
            pltpu.VMEM((taps // UNIT + 1, UNIT, UNIT), jnp.bfloat16),
            pltpu.VMEM((slots, GROUP, regions), jnp.float32),
            pltpu.VMEM((2, slots // 2, comps * moves, GROUP, UNIT), jnp.float32),
            pltpu.VMEM((comps, taps // UNIT, GROUP * moves * templates, UNIT), jnp.float32),
            pltpu.VMEM((record // UNIT, 16 * (comps * stations + 1), UNIT), jnp.float32),
            pltpu.VMEM((taps // UNIT, width // UNIT + 1, comps * stations, UNIT), jnp.float32),
            pltpu.VMEM((taps // UNIT, piece // UNIT + 1, templates, UNIT), jnp.float32),
            pltpu.SemaphoreType.DMA((5 + taps // UNIT,)),
            pltpu.SemaphoreType.DMA((pieces - 1,)),
            pltpu.SemaphoreType.DMA((pieces - 1,)),
            pltpu.SemaphoreType.DMA((pieces - 1,)),
            pltpu.SemaphoreType.DMA,
            pltpu.SemaphoreType.DMA,
        ],
        compiler_params=pltpu.CompilerParams(collective_id=0, has_side_effects=True,
                                             vmem_limit_bytes=50 << 20),
        name="matched",
    )(*[x if x.size == 1 else pltpu.with_memory_space_constraint(x, pltpu.HBM) for x in (
        jnp.transpose(waveforms, (1, 0, 2)), jnp.transpose(tail, (1, 0, 2)), station_lists.T,
        station_count, bank_of_region, bank_rows, jnp.transpose(moveouts, (2, 0, 1)))])


def solution(mesh):
    return jax.shard_map(
        on_device,
        mesh=mesh,
        in_specs=(
            P("grp", None, "reg"),
            P("grp", None, None),
            P("grp", None),
            P(("grp", "reg")),
            P(("grp", "reg")),
            P(),
            P(("grp", "reg"), None, None),
        ),
        out_specs=P("grp", "reg"),
        check_vma=False,
    )
```

```python
import functools
import math

import jax
import jax.numpy as jnp
from jax import lax
from jax.experimental import pallas as pl
from jax.experimental.pallas import tpu as pltpu
from jax.sharding import PartitionSpec as P

UNIT = 128
GROUP = 16
SPAN = 8
MESH = pl.DeviceIdType.MESH


def lay(blocks, width):
    if width % UNIT == 0:
        return jnp.concatenate(blocks, axis=1)
    per = UNIT // width
    tiles = []
    for start in range(0, len(blocks), per):
        tile = blocks[start]
        for i, block in enumerate(blocks[start + 1:start + per]):
            tile = tile + pltpu.roll(block, (i + 1) * width, 1)
        tiles.append(tile)
    return jnp.concatenate(tiles, axis=1)


def padded(x, lanes):
    if x.shape[1] % lanes == 0:
        return x
    return jnp.concatenate([x, jnp.zeros((x.shape[0], lanes - x.shape[1] % lanes), x.dtype)], axis=1)


def kernel(n, taps, scale, wave_hbm, tail_hbm, lists_hbm, count_hbm, bank_hbm, lib_hbm, mov_hbm, out_ref,
           rec, lists, count, bank, lib, mov, mine, meta, spread, band, member, tally, summed, fans, gain, partial,
           local, tails, halo_send, halo_recv, meta_send, meta_recv):
    me = lax.axis_index("reg")
    pieces, comps, stations, piece = rec.shape
    halos = pieces - 1
    record = pieces * piece
    channels, _, templates = mov.shape
    slots, regions = lists.shape
    quarters = taps // UNIT
    banks = lib.shape[1] // channels
    moves = (record - piece - taps) // UNIT + 1
    width = piece + (moves - 1) * UNIT
    pitch = comps * stations + 1
    packs = UNIT // templates
    sides = slots // 2
    half = templates // 2
    groups = stations // GROUP

    barrier = pltpu.get_barrier_semaphore()
    loads = [pltpu.make_async_copy(src, dst, local.at[i]) for i, (src, dst) in enumerate(
        [(mov_hbm, mov), (count_hbm, count), (bank_hbm, bank), (lists_hbm, lists), (wave_hbm, rec.at[0])]
        + [(lib_hbm.at[:, :, j * UNIT:(j + 1) * UNIT], lib.at[j]) for j in range(quarters)])]

    @pl.loop(1, n)
    def _(step):
        pl.semaphore_signal(barrier, inc=1, device_id={"reg": lax.rem(me + step, n)}, device_id_type=MESH)

    for copy in loads[:5]:
        copy.start()

    def tail_copy(h, q):
        return pltpu.make_async_copy(tail_hbm.at[:, :, pl.ds(q * piece, piece)], rec.at[h], tails.at[h - 1])

    for h in range(1, halos + 1):
        for q in range(h):
            @pl.when(me + h - n == q)
            def _():
                tail_copy(h, q).start()

    for copy in loads[5:]:
        copy.start()
    for copy in loads[:3]:
        copy.wait()
    lane = lax.broadcasted_iota(jnp.int32, (1, UNIT), 1)
    live = jnp.broadcast_to(count[...].reshape(1, 1), (1, UNIT))
    for q in range(2):
        spots = []
        for i in range(packs):
            if i < sides * comps:
                c = (q * sides + i // comps) * comps + i % comps
                row = padded(mov[c], UNIT)
                spots.append(jnp.where(lane < templates, jnp.where(c // comps < live, row, moves), 0))
            else:
                spots.append(jnp.where(lane < templates, jnp.broadcast_to(bank[...].reshape(1, 1), (1, UNIT)), 0))
        mine[q:q + 1] = lay(spots, templates)

    def meta_copy(step):
        return pltpu.make_async_remote_copy(
            src_ref=mine, dst_ref=meta.at[me], send_sem=meta_send, recv_sem=meta_recv,
            device_id={"reg": lax.rem(me + step, n)}, device_id_type=MESH)

    def halo_copy(h):
        return pltpu.make_async_remote_copy(
            src_ref=rec.at[0], dst_ref=rec.at[h], send_sem=halo_send.at[h - 1], recv_sem=halo_recv.at[h - 1],
            device_id={"reg": lax.rem(me + n - h, n)}, device_id_type=MESH)

    for copy in loads[3:5]:
        copy.wait()

    def choose(base):
        station = lax.broadcasted_iota(jnp.int32, (GROUP, regions), 0) + base
        for k in range(slots):
            here = jnp.broadcast_to(lists[k:k + 1], station.shape) == station
            member[k] = jnp.where(here, 1.0, 0.0)

    if groups == 1:
        choose(0)

    pl.semaphore_wait(barrier, n - 1)

    @pl.loop(1, n)
    def _(step):
        meta_copy(step).start()

    for h in range(1, halos + 1):
        @pl.when(me >= h)
        def _():
            halo_copy(h).start()

    meta[me] = mine[...]
    source = lax.broadcasted_iota(jnp.int32, (UNIT, UNIT), 0)
    target = lax.broadcasted_iota(jnp.int32, (UNIT, UNIT), 1)
    for i in range(packs):
        part = target // (UNIT // 2) if i // comps % 2 == 0 else 1 - target // (UNIT // 2)
        spread[i] = jnp.where(source == target % half + part * half + i * templates, 1.0, 0.0).astype(jnp.bfloat16)
    for i in range(quarters + 1):
        full = jnp.ones((UNIT, UNIT), jnp.float32)
        full = jnp.where(source >= target, full, 0.0) if i == 0 else full
        full = jnp.where(source < target, full, 0.0) if i == quarters else full
        band[i] = full.astype(jnp.bfloat16)
    for copy in loads[5:]:
        copy.wait()
    chunk = lax.broadcasted_iota(jnp.int32, (templates, UNIT), 1) // (UNIT // quarters)

    def reorder(e):
        now = [lib[j, e] for j in range(quarters)]
        bit = quarters // 2
        while bit:
            first = chunk // bit % 2 == 0
            reach = bit * (UNIT // quarters)
            then = list(now)
            for j in range(quarters):
                if not j & bit:
                    then[j] = jnp.where(first, now[j], pltpu.roll(now[j + bit], reach, 1))
                    then[j + bit] = jnp.where(first, pltpu.roll(now[j], UNIT - reach, 1), now[j + bit])
            now = then
            bit //= 2
        return now

    @pl.loop(0, banks // 2)
    def _(g):
        @pl.loop(0, channels, unroll=6)
        def _(c):
            at = g * (2 * channels) + c
            first, second = reorder(at), reorder(at + channels)
            for j in range(quarters):
                lib[j, at] = jnp.concatenate([first[j][:half], second[j][:half]], axis=0)
                lib[j, at + channels] = jnp.concatenate([first[j][half:], second[j][half:]], axis=0)

    everyone = meta.at[pl.ds(0, n - 1)]
    pltpu.make_async_copy(everyone, everyone, meta_recv).wait()

    for h in range(1, halos + 1):
        for q in range(h):
            @pl.when(me + h - n == q)
            def _():
                tail_copy(h, q).wait()

        @pl.when(me + h < n)
        def _():
            halo_copy(h).wait_recv()

    told = jnp.concatenate([meta[:, q, :] for q in range(2)], axis=0).astype(jnp.float32).astype(jnp.bfloat16)
    tiled = jnp.dot(told, jnp.concatenate([spread[i] for i in range(packs)], axis=1), preferred_element_type=jnp.float32)

    def facts(q, i):
        return tiled[q * regions:(q + 1) * regions, i * UNIT:(i + 1) * UNIT]

    wide = lax.broadcasted_iota(jnp.int32, (regions, UNIT), 1) // half % banks
    home = facts(0, sides * comps) == wide.astype(jnp.float32)

    def unfold(s):
        s = s if stations == 16 else pl.multiple_of(s, 16)
        squares = []
        for c in range(comps):
            x = jnp.concatenate([rec[p, c, pl.ds(s, 16)] for p in range(pieces)], axis=1).astype(jnp.float32)
            for k in range(16):
                moved = pltpu.roll(x, record - k, 1) if k else x
                for j in range(fans.shape[0]):
                    fans[j, pl.ds(k * pitch + c * stations + s, 16)] = moved[:, j * UNIT:(j + 1) * UNIT]
            square = x * x
            big = square.astype(jnp.bfloat16)
            squares.append((big, (square - big.astype(jnp.float32)).astype(jnp.bfloat16)))
        both = jnp.concatenate([part[i] for i in range(2) for part in squares], axis=0)
        energy = jnp.dot(
            jnp.concatenate([both[:, a * UNIT:(a + quarters + 1) * UNIT] for a in range(width // UNIT)], axis=0),
            jnp.concatenate([band[i] for i in range(quarters + 1)], axis=0), preferred_element_type=jnp.float32)
        half = 16 * comps
        levels = []
        for a in range(width // UNIT):
            total = energy[2 * a * half:(2 * a + 1) * half] + energy[(2 * a + 1) * half:(2 * a + 2) * half]
            levels.append(lax.rsqrt(total / taps + 1e-05) * scale)
        level = jnp.concatenate(levels + levels[:1], axis=1)
        for i in range(quarters):
            moved = pltpu.roll(level, i * (UNIT // quarters), 1) if i else level
            for c in range(comps):
                for b in range(gain.shape[1]):
                    gain[i, b, pl.ds(c * stations + s, 16)] = moved[c * 16:(c + 1) * 16, b * UNIT:(b + 1) * UNIT]

    if stations == 16:
        unfold(0)
    else:
        pl.loop(0, stations, step=16)(unfold)

    def combine():
        left = lax.broadcasted_iota(jnp.int32, (GROUP, UNIT), 1) < UNIT // 2
        for p in range(slots // 2):
            many = []
            for k in (2 * p, 2 * p + 1):
                parts = []
                for c in range(comps):
                    q, side = divmod(k, sides)
                    shift = jnp.where(home, facts(q, side * comps + c), float(moves))
                    for m in range(moves):
                        parts.append(jnp.where(shift == m, 1.0, 0.0).astype(jnp.bfloat16))
                many.append(jnp.dot(member[k].astype(jnp.bfloat16), jnp.concatenate(parts, axis=1),
                                    preferred_element_type=jnp.float32))
            for i in range(comps * moves):
                even, odd = [one[:, i * UNIT:(i + 1) * UNIT] for one in many]
                tally[0, p, i] = jnp.where(left, even, odd)
                tally[1, p, i] = jnp.where(left, odd, even)
        own = (lax.broadcasted_iota(jnp.int32, (half, UNIT), 1) % half
               == lax.broadcasted_iota(jnp.int32, (half, UNIT), 0))

        for c in range(comps):
            for h in range(2):
                picks = [jnp.concatenate([
                    jnp.where(own, jnp.broadcast_to(tally[h, p, c * moves + m, s:s + 1], own.shape), 0.0)
                    for p in range(slots // 2)], axis=1) for s in range(GROUP) for m in range(moves)]
                weights = jnp.concatenate([
                    jnp.concatenate([lib[j, (2 * g + h) * channels + (2 * p + (side ^ h)) * comps + c]
                                     for j in range(quarters)], axis=1)
                    for p in range(slots // 2) for side in range(2) for g in range(banks // 2)], axis=0)
                total = jnp.dot(jnp.concatenate(picks, axis=0).astype(jnp.bfloat16), weights,
                                preferred_element_type=jnp.float32)
                for j in range(quarters):
                    for i in range(GROUP * moves):
                        to = i * templates + h * half
                        summed[c, j, to:to + half] = total[i * half:(i + 1) * half, j * UNIT:(j + 1) * UNIT]

    if groups == 1:
        combine()

    across = piece // UNIT

    def correlate(c, s, within, totals):
        low = jnp.concatenate([fans[j, pl.ds(c * stations + s, 16, stride=pitch)]
                               for j in range(fans.shape[0])], axis=1).astype(jnp.bfloat16)
        high = pltpu.roll(low, record - 16, 1)

        def signal(first, count):
            rows = [part[:, (j + first) * UNIT:(j + first + count) * UNIT] for j in range(quarters) for part in (low, high)]
            return jnp.concatenate(rows + rows, axis=0)

        kernels = []
        for m in range(moves):
            at = pl.multiple_of((within * moves + m) * templates, templates)
            for i in range(quarters):
                whole = summed[c, i, pl.ds(at, templates)]
                big = whole.astype(jnp.bfloat16)
                small = (whole - big.astype(jnp.float32)).astype(jnp.bfloat16)
                kernels.append(jnp.concatenate([big, small], axis=1))
        for first, count in ((0, 2), (2, 1), (3, 2)):
            wanted = [(m, i, q) for m in range(moves) for i in range(quarters)
                      for q in [[b for b in range(first, first + count) if 0 <= b - m < across + (i > 0)]] if q]
            corr = jnp.dot(jnp.concatenate([kernels[m * quarters + i] for m, i, _ in wanted], axis=0),
                           signal(first, count), preferred_element_type=jnp.float32)
            for at, (m, i, q) in enumerate(wanted):
                for b in q:
                    one = corr[at * templates:(at + 1) * templates, (b - first) * UNIT:(b - first + 1) * UNIT]
                    one = one * gain[i, b, pl.ds(c * stations + s, 1)]
                    old = totals.get((i, b - m))
                    totals[i, b - m] = one if old is None else old + one

    partial[...] = jnp.zeros_like(partial)

    @pl.loop(0, groups)
    def _(g):
        if groups > 1:
            choose(g * GROUP)
            combine()

        @pl.loop(0, GROUP, step=SPAN)
        def _(within):
            totals = {}
            for i in range(SPAN):
                for c in range(comps):
                    correlate(c, g * GROUP + within + i, within + i, totals)
            for (i, q), total in totals.items():
                partial[i, q] += total

    result = None
    for i in range(quarters):
        whole = jnp.concatenate([partial[i, q] for q in range(across + 1)], axis=1)
        whole = pltpu.roll(whole, whole.shape[1] - i * (UNIT // quarters), 1) if i else whole
        result = whole if result is None else result + whole
    out_ref[...] = result[:, 0:piece]

    for h in range(1, halos + 1):
        @pl.when(me >= h)
        def _():
            halo_copy(h).wait_send()

    pltpu.make_async_copy(everyone, everyone, meta_send).wait()


def on_device(waveforms, tail, station_lists, station_count, bank_of_region, library, moveouts):
    n = lax.axis_size("reg")
    stations, comps, piece = waveforms.shape
    banks, templates, channels, taps = library.shape
    regions, slots = station_lists.shape
    scale = 1.0 / math.sqrt(comps * slots * regions)
    pieces = 1 + tail.shape[2] // piece
    record = pieces * piece
    moves = (record - piece - taps) // UNIT + 1
    width = record - taps
    packs = UNIT // templates
    bank_rows = jnp.transpose(library, (0, 2, 1, 3)).reshape(banks * channels, templates, taps)
    anywhere = pl.BlockSpec(memory_space=pltpu.HBM)
    return pl.pallas_call(
        functools.partial(kernel, n, taps, scale),
        out_shape=jax.ShapeDtypeStruct((templates, piece), jnp.float32),
        in_specs=[anywhere] * 7,
        out_specs=pl.BlockSpec(memory_space=pltpu.VMEM),
        scratch_shapes=[
            pltpu.VMEM((pieces, comps, stations, piece), jnp.bfloat16),
            pltpu.VMEM((slots, regions), jnp.int32),
            pltpu.VMEM((1,), jnp.int32),
            pltpu.VMEM((1,), jnp.int32),
            pltpu.VMEM((taps // UNIT, banks * channels, templates, UNIT), library.dtype),
            pltpu.VMEM((channels, 1, templates), jnp.int32),
            pltpu.VMEM((2, UNIT), jnp.int32),
            pltpu.VMEM((n, 2, UNIT), jnp.int32),
            pltpu.VMEM((packs, UNIT, UNIT), jnp.bfloat16),
            pltpu.VMEM((taps // UNIT + 1, UNIT, UNIT), jnp.bfloat16),
            pltpu.VMEM((slots, GROUP, regions), jnp.float32),
            pltpu.VMEM((2, slots // 2, comps * moves, GROUP, UNIT), jnp.float32),
            pltpu.VMEM((comps, taps // UNIT, GROUP * moves * templates, UNIT), jnp.float32),
            pltpu.VMEM((record // UNIT, 16 * (comps * stations + 1), UNIT), jnp.float32),
            pltpu.VMEM((taps // UNIT, width // UNIT + 1, comps * stations, UNIT), jnp.float32),
            pltpu.VMEM((taps // UNIT, piece // UNIT + 1, templates, UNIT), jnp.float32),
            pltpu.SemaphoreType.DMA((5 + taps // UNIT,)),
            pltpu.SemaphoreType.DMA((pieces - 1,)),
            pltpu.SemaphoreType.DMA((pieces - 1,)),
            pltpu.SemaphoreType.DMA((pieces - 1,)),
            pltpu.SemaphoreType.DMA,
            pltpu.SemaphoreType.DMA,
        ],
        compiler_params=pltpu.CompilerParams(collective_id=0, has_side_effects=True,
                                             vmem_limit_bytes=50 << 20),
        name="matched",
    )(*[x if x.size == 1 else pltpu.with_memory_space_constraint(x, pltpu.HBM) for x in (
        jnp.transpose(waveforms, (1, 0, 2)), jnp.transpose(tail, (1, 0, 2)), station_lists.T,
        station_count, bank_of_region, bank_rows, jnp.transpose(moveouts, (2, 0, 1)))])


def solution(mesh):
    return jax.shard_map(
        on_device,
        mesh=mesh,
        in_specs=(
            P("grp", None, "reg"),
            P("grp", None, None),
            P("grp", None),
            P(("grp", "reg")),
            P(("grp", "reg")),
            P(),
            P(("grp", "reg"), None, None),
        ),
        out_specs=P("grp", "reg"),
        check_vma=False,
    )
```
